128 devices in a mesh: row: 8 (over z, core), col: 16 (over y, x).
Axes of the slice: x: 4, y: 4, z: 4, core: 2. Of those that a mesh axis runs over, the one named last changes fastest.
Arguments:
- front_panel: float32 [12288, 1024], P('row', 'col')
- front_trail: float32 [12288, 8192], P('row', 'col'), may hold values from -6 to 6
- child_panel: float32 [2, 8192, 1024], P(None, 'row', 'col'), may hold values from -0.1875 to 0.1875
- child_trail: float32 [2, 8192, 8192], P(None, 'row', 'col'), may hold values from -4 to 4
- child_map: int32 [2, 8192], P(None, 'row'), may hold values from 0 to 1535, as said below
- child_count: int32 [2, 8], P(None, 'row'), may hold values from 256 to 1024, as said below
Outputs:
- factor: float32 [12288, 1024], P('row', 'col')
- schur_block: float32 [12288, 8192], P('row', 'col')
The draws below stay inside these ranges and needn't reach their ends.
Inputs may be any that keep to these rules, and one draw needn't show every extreme that they name: `child_map`: within each slab and each aligned block of 1024 entries the values are distinct rows of one row block. `child_count`: some slab of some row block has all 1024 rows live in every draw.
All inputs are finite; a program needn't handle non-finite values.
Results may differ from the reference program's by a relative error of at most 0.00012.
Values sent between devices are 32-bit elements; how exact they have to be, the bound alone decides.
No kernel may reach another device: no remote copies, remote signals or barrier semaphores. Data moves between devices by JAX's collectives and lax.ppermute only.
A program may use at most 192 MiB of HBM per device.

```python
import math
import jax
import jax.numpy as jnp
from jax import lax

F = 12288
PB = 1024
CR = 1024
FR = 1536
TW = 8192
CHILD_ROWS = 8192
N_ROW = 8


def draw_front_panel(key, part):
    key_noise, key_diag = jax.random.split(jax.random.fold_in(key, 11), 2)
    row_index = jnp.arange(F)[:, None]
    col_index = jnp.arange(PB)[None, :]
    noise = jax.random.normal(key_noise, (F, PB), jnp.float32)
    diag_values = jax.random.uniform(key_diag, (F, PB), jnp.float32, 8.0, 12.0)
    in_diag = row_index < PB
    block_values = jnp.where(row_index == col_index, diag_values, noise * (2.0 / math.sqrt(PB)))
    return jnp.where(in_diag, block_values, noise).astype(jnp.float32)


def draw_child_map(key, part):
    all_keys = jax.random.split(jax.random.fold_in(key, 23), 2 * N_ROW)
    picked = jax.vmap(lambda one_key: jax.random.permutation(one_key, FR)[:CR])(all_keys)
    return picked.reshape(2, N_ROW * CR).astype(jnp.int32)


def draw_child_count(key, part):
    key_counts, key_pick = jax.random.split(jax.random.fold_in(key, 37))
    counts = jax.random.randint(key_counts, (2 * N_ROW,), CR // 4, CR + 1)
    chosen = jax.random.randint(key_pick, (), 0, 2 * N_ROW)
    filled = jnp.where(jnp.arange(2 * N_ROW) == chosen, CR, counts)
    return filled.reshape(2, N_ROW).astype(jnp.int32)


def block_levels(key, dims, shards, least, top_value):
    loudness, own = 1.0, jax.random.fold_in(key, 6)
    for axis_at, blocks in shards:
        heights = jnp.exp(jax.random.uniform(jax.random.fold_in(own, axis_at), (blocks,), jnp.float32, least / len(shards), top_value / len(shards)))
        loudness = loudness * jnp.repeat(heights, dims[axis_at] // blocks).reshape([-1 if axis == axis_at else 1 for axis in range(len(dims))])
    return loudness


def centred(rng, shape, deviation, bound, pieces=(), kind=jnp.bfloat16):
    loudness = block_levels(rng, shape, pieces, -0.22, 0.18) if pieces else 1.0
    result = jax.random.normal(rng, shape, jnp.float32) * deviation * loudness
    return jnp.minimum(jnp.maximum(result, -bound), bound).astype(kind)


def setup_inputs(seed: int = 0) -> dict:
    seeds = jax.random.split(jax.random.key(seed), 7)
    front_panel = draw_front_panel(jax.random.fold_in(seeds[6], 71), 0)
    front_trail = centred(seeds[1], (F, TW), 1.0, 6.0, ((0, 8), (1, 16)), jnp.float32)
    child_panel = centred(seeds[2], (2, CHILD_ROWS, PB), PB ** -0.5, 0.1875, ((1, 8), (2, 16)), jnp.float32)
    child_trail = centred(seeds[3], (2, CHILD_ROWS, TW), 0.25, 4.0, ((1, 8), (2, 16)), jnp.float32)
    child_map = draw_child_map(jax.random.fold_in(seeds[6], 71), 0)
    child_count = draw_child_count(jax.random.fold_in(seeds[6], 71), 0)
    return dict(front_panel=front_panel, front_trail=front_trail, child_panel=child_panel, child_trail=child_trail, child_map=child_map, child_count=child_count)


def reference(front_panel, front_trail, child_panel, child_trail, child_map, child_count):
    front_window = jnp.concatenate([front_panel, front_trail], axis=1)
    child_slabs = jnp.concatenate([child_panel, child_trail], axis=2)
    positions = jnp.arange(N_ROW * CR, dtype=jnp.int32)
    source_block = positions // CR
    within = positions - source_block * CR
    for slab_index in range(2):
        if slab_index == 0:
            target_block = source_block
        else:
            target_block = jnp.bitwise_xor(source_block, N_ROW // 2)
        counts = child_count[slab_index][source_block]
        target = jnp.where(within < counts, target_block * FR + child_map[slab_index], F).astype(jnp.int32)
        front_window = front_window.at[target].add(child_slabs[slab_index], mode='drop')
    assembled_panel = front_window[:, :PB]
    assembled_trail = front_window[:, PB:]
    diag_block = assembled_panel[:PB]
    symmetric = 0.5 * (diag_block + diag_block.T)
    lower_factor = jnp.linalg.cholesky(symmetric)
    solved = jax.scipy.linalg.solve_triangular(lower_factor, assembled_panel.T, lower=True).T
    factor = jnp.concatenate([lower_factor, solved[PB:]], axis=0)
    window_factor = factor[PB:PB + TW]
    schur_block = assembled_trail - jnp.dot(factor, window_factor.T, precision=lax.Precision.HIGHEST)
    return (factor, schur_block)
```

```python
import jax
import jax.numpy as jnp
from jax import lax
from jax.experimental import pallas as pl
from jax.experimental.pallas import tpu as pltpu
from jax.sharding import PartitionSpec as P

f32 = jnp.float32
bf16 = jnp.bfloat16

F = 12288
PB = 1024
CR = 1024
FR = 1536
TC = 512
PC = 64
B = 128
NB = PB // B
Q = 256
MB = 1 << 20

NATURAL = (((1,), (0,)), ((), ()))
LHS_T = (((0,), (0,)), ((), ()))
RHS_T = (((1,), (1,)), ((), ()))


def split(x):
    hi = x.astype(bf16)
    return hi, (x - hi.astype(f32)).astype(bf16)


def dot1(a, b, dims=NATURAL):
    return lax.dot_general(a, b, dims, preferred_element_type=f32)


def dot3(a, b, dims=NATURAL):
    (ah, al), (bh, bl) = a, b
    return dot1(ah, bh, dims) + (dot1(ah, bl, dims) + dot1(al, bh, dims))


def one_hot(first, rows, target):
    at = first + lax.broadcasted_iota(jnp.int32, (rows, CR), 0)
    return (at == target).astype(f32).astype(bf16)


def live_target(count, map_row):
    k = lax.broadcasted_iota(jnp.int32, (1, CR), 1)
    return jnp.where(k < count, map_row, -1)


def panel_kernel(count_ref, map_ref, front_ref, child_ref, own_ref, send_ref):
    for slab in range(2):
        target = live_target(count_ref[slab, 0], map_ref[slab:slab + 1, :])
        c = child_ref[slab]
        hi = c.astype(bf16)
        rest = c - hi.astype(f32)
        mid = rest.astype(bf16)
        low = (rest - mid.astype(f32)).astype(bf16)
        parts = jnp.concatenate([hi, mid, low], axis=0)
        for at in range(0, FR, 512):
            moved = dot1(parts, one_hot(at, 512, target), RHS_T)
            moved = moved[:PC] + (moved[PC:2 * PC] + moved[2 * PC:])
            if slab == 0:
                own_ref[:, at:at + 512] = front_ref[:, at:at + 512] + moved
            else:
                send_ref[:PC, at:at + 512] = moved
        if slab == 1:
            send_ref[PC:, :CR] = jnp.broadcast_to(target.astype(f32), (8, CR))
            send_ref[PC:, CR:] = jnp.zeros((8, FR - CR), f32)


def panel_parts(count, child_map, front_t, child_t):
    return pl.pallas_call(
        panel_kernel,
        name="panel_parts",
        out_shape=(jax.ShapeDtypeStruct((PC, FR), f32), jax.ShapeDtypeStruct((PC + 8, FR), f32)),
        in_specs=[pl.BlockSpec(memory_space=pltpu.SMEM)] + [pl.BlockSpec(memory_space=pltpu.VMEM)] * 3,
        out_specs=(pl.BlockSpec(memory_space=pltpu.VMEM),) * 2,
        compiler_params=pltpu.CompilerParams(vmem_limit_bytes=24 * MB),
    )(count, child_map, front_t, child_t)


def trail_kernel(count_ref, map_ref, front_ref, child_ref, out_ref, ch, cl):
    @pl.when(pl.program_id(0) == 0)
    def _():
        ch[...], cl[...] = split(child_ref[...])

    target = live_target(count_ref[0, 0], map_ref[0:1, :])
    g = one_hot(pl.program_id(0) * 512, 512, target)
    out_ref[...] = front_ref[...] + (dot1(g, ch[...]) + dot1(g, cl[...]))


def trail_own(count, child_map, front, child):
    return pl.pallas_call(
        trail_kernel,
        name="trail_own",
        grid=(FR // 512,),
        out_shape=jax.ShapeDtypeStruct((FR, TC), f32),
        in_specs=[
            pl.BlockSpec(memory_space=pltpu.SMEM),
            pl.BlockSpec((2, CR), lambda s: (0, 0)),
            pl.BlockSpec((512, TC), lambda s: (s, 0)),
            pl.BlockSpec((None, CR, TC), lambda s: (0, 0, 0)),
        ],
        out_specs=pl.BlockSpec((512, TC), lambda s: (s, 0)),
        scratch_shapes=[pltpu.VMEM((CR, TC), bf16)] * 2,
        compiler_params=pltpu.CompilerParams(vmem_limit_bytes=24 * MB),
    )(count, child_map, front, child)


def lane(x, at):
    return jnp.broadcast_to(x[:, at:at + 1], (8, B))


def chain(w_ref):
    def rows(r):
        x = jnp.broadcast_to(w_ref[r:r + 1, :], (8, 2 * B))
        return x[:, :B], x[:, B:]

    for q in range(4):
        done = []
        for t in range(4):
            m = 4 * q + t
            p, a = [], []
            for i in range(8):
                x, y = rows(8 * m + i)
                p.append(x)
                a.append(y)

            def apply(u):
                b = [[lane(u[j][0], 8 * m + i) for j in range(8)] for i in range(8)]
                for i in range(8):
                    for j in range(8):
                        p[i] = p[i] - b[i][j] * u[j][0]
                        a[i] = a[i] - b[i][j] * u[j][1]
                return b

            for u in done[:-1]:
                apply(u)
            d = {(i, j): lane(p[i], 8 * m + j) for i in range(8) for j in range(i + 1)}
            if done:
                b = apply(done[-1])
                for i in range(8):
                    for j in range(i + 1):
                        for k in range(8):
                            d[i, j] = d[i, j] - b[i][k] * b[j][k]
            u = []
            for j in range(8):
                r = lax.rsqrt(d[j, j])
                low = {i: d[i, j] * r for i in range(j + 1, 8)}
                for i in range(j + 1, 8):
                    for k in range(j + 1, i + 1):
                        d[i, k] = d[i, k] - low[i] * low[k]
                uj, vj = p[j] * r, a[j] * r
                u.append((uj, vj))
                for i in range(j + 1, 8):
                    p[i] = p[i] - low[i] * uj
                    a[i] = a[i] - low[i] * vj
            sub = lax.broadcasted_iota(jnp.int32, (8, B), 0)
            cu, cv = u[0]
            for j in range(1, 8):
                cu = jnp.where(sub == j, u[j][0], cu)
                cv = jnp.where(sub == j, u[j][1], cv)
            w_ref[8 * m:8 * m + 8, :B] = cu
            w_ref[8 * m:8 * m + 8, B:] = cv
            done.append(u)
        if q < 3:
            um = w_ref[32 * q:32 * q + 32, :]
            ut = um[:, :B].T[32 * (q + 1):, :]
            w_ref[32 * (q + 1):, :] = w_ref[32 * (q + 1):, :] - dot3(split(ut), split(um))


def chol_kernel(at_ref, d_ref, uh, ul, lh, ll, ih, il, s_ref, w_ref, v_ref):
    col = at_ref[1]
    for j in range(PB // PC):
        s_ref[PC * j:PC * (j + 1), :] = d_ref[jnp.bitwise_xor(col, j)]
    for i in range(NB):
        for j in range(i, NB):
            up = s_ref[i * B:(i + 1) * B, j * B:(j + 1) * B]
            dn = s_ref[j * B:(j + 1) * B, i * B:(i + 1) * B]
            s_ref[i * B:(i + 1) * B, j * B:(j + 1) * B] = 0.5 * (up + dn.T)
    r = lax.broadcasted_iota(jnp.int32, (B, B), 0)
    c = lax.broadcasted_iota(jnp.int32, (B, B), 1)
    eye = (r == c).astype(f32)

    def step(k, _):
        for kk in range(NB):
            @pl.when(k == kk)
            def _():
                here = slice(kk * B, (kk + 1) * B)
                if kk:
                    left = (lh[here, :kk * B], ll[here, :kk * B])
                    right = (uh[:kk * B, kk * B:], ul[:kk * B, kk * B:])
                    s_ref[here, kk * B:] = s_ref[here, kk * B:] - dot3(left, right)
                w_ref[:, :B] = s_ref[here, here]

        w_ref[:, B:] = eye
        chain(w_ref)
        v = w_ref[:, B:]
        v_ref[k % 2] = v
        vs = split(v)
        for kk in range(NB):
            @pl.when(k == kk)
            def _():
                here = slice(kk * B, (kk + 1) * B)
                rest = slice((kk + 1) * B, PB)
                dh, dl = split(jnp.where(r <= c, w_ref[:, :B], 0.0))
                uh[here, here] = dh
                ul[here, here] = dl
                if kk:
                    uh[here, :kk * B] = jnp.zeros((B, kk * B), bf16)
                    ul[here, :kk * B] = jnp.zeros((B, kk * B), bf16)
                if kk < NB - 1:
                    rh, rl = split(dot3(vs, split(s_ref[here, rest])))
                    uh[here, rest] = rh
                    ul[here, rest] = rl
                    lh[rest, here] = rh.T
                    ll[rest, here] = rl.T
                half = kk % 2
                at = half * B
                ih[kk // 2, at:at + B, at:at + B] = vs[0]
                il[kk // 2, at:at + B, at:at + B] = vs[1]
                if half:
                    before = slice((kk - 1) * B, kk * B)
                    first = split(v_ref[0])
                    cross = split(dot3((lh[here, before], ll[here, before]), first))
                    th, tl = split(-dot3(vs, cross))
                    ih[kk // 2, B:, :B] = th
                    il[kk // 2, B:, :B] = tl
                    ih[kk // 2, :B, B:] = jnp.zeros((B, B), bf16)
                    il[kk // 2, :B, B:] = jnp.zeros((B, B), bf16)
        return 0

    lax.fori_loop(0, NB, step, 0)


def cholesky(at, pieces):
    full = jax.ShapeDtypeStruct((PB, PB), bf16)
    inv = jax.ShapeDtypeStruct((PB // Q, Q, Q), bf16)
    return pl.pallas_call(
        chol_kernel,
        name="chol",
        out_shape=(full,) * 4 + (inv,) * 2,
        in_specs=[pl.BlockSpec(memory_space=pltpu.SMEM), pl.BlockSpec(memory_space=pltpu.VMEM)],
        out_specs=(pl.BlockSpec(memory_space=pltpu.VMEM),) * 6,
        scratch_shapes=[
            pltpu.VMEM((PB, PB), f32),
            pltpu.VMEM((B, 2 * B), f32),
            pltpu.VMEM((2, B, B), f32),
        ],
        compiler_params=pltpu.CompilerParams(vmem_limit_bytes=40 * MB),
    )(at, pieces)


def finish_kernel(at_ref, win_ref, pan_ref, tgt_ref, trail_ref, child_ref, uh, ul, lh, ll, ih, il,
                  fac_ref, out_ref, a_ref, xh, xl, wh, wl, ch, cl):
    s = pl.program_id(0)
    row = at_ref[0]
    col = at_ref[1]

    def solve(yh, yl):
        for k in range(PB // Q):
            here = slice(k * Q, (k + 1) * Q)
            v = a_ref[here, :]
            if k:
                v = v - dot3((lh[here, :k * Q], ll[here, :k * Q]), (yh[:k * Q, :], yl[:k * Q, :]))
            yh[here, :], yl[here, :] = split(dot3((ih[k], il[k]), split(v)))

    @pl.when(s == 0)
    def _():
        for j in range(8):
            a_ref[B * j:B * (j + 1), :] = win_ref[jnp.bitwise_xor(row, j)]
        solve(wh, wl)
        ch[...], cl[...] = split(child_ref[...])

    @pl.when(s > 0)
    def _():
        own = jnp.logical_and(row == 0, s < 3)

        @pl.when(own)
        def _():
            here = pl.ds(pl.multiple_of((s - 1) * 512, 512), 512)
            xh[...] = uh[:, here]
            xl[...] = ul[:, here]

        @pl.when(jnp.logical_not(own))
        def _():
            a_ref[...] = pan_ref[...]
            solve(xh, xl)

        mine = pl.ds(pl.multiple_of(col * PC, PC), PC)
        fac_ref[...] = xh[mine, :].astype(f32) + xl[mine, :].astype(f32)
        target = tgt_ref[PC:PC + 1, :CR].astype(jnp.int32)
        g = one_hot((s - 1) * 512, 512, target)
        moved = dot1(g, ch[...]) + dot1(g, cl[...])
        prod = dot3((xh[...], xl[...]), (wh[...], wl[...]), LHS_T)
        out_ref[...] = trail_ref[...] + (moved - prod)


def finish(at, window, panel, got, trail, child, factors):
    def back(s):
        return jnp.maximum(s - 1, 0)

    whole = lambda shape: pl.BlockSpec(shape, lambda s: (0,) * len(shape), pipeline_mode=pl.Buffered(1))
    return pl.pallas_call(
        finish_kernel,
        name="finish",
        grid=(1 + FR // 512,),
        out_shape=(jax.ShapeDtypeStruct((PC, FR), f32), jax.ShapeDtypeStruct((FR, TC), f32)),
        in_specs=[
            pl.BlockSpec(memory_space=pltpu.SMEM),
            whole((8, B, TC)),
            pl.BlockSpec((PB, 512), lambda s: (0, back(s))),
            whole((PC + 8, FR)),
            pl.BlockSpec((512, TC), lambda s: (back(s), 0)),
            whole((CR, TC)),
            whole((PB, PB)), whole((PB, PB)), whole((PB, PB)), whole((PB, PB)),
            whole((PB // Q, Q, Q)), whole((PB // Q, Q, Q)),
        ],
        out_specs=(
            pl.BlockSpec((PC, 512), lambda s: (0, back(s))),
            pl.BlockSpec((512, TC), lambda s: (back(s), 0)),
        ),
        scratch_shapes=[pltpu.VMEM((PB, TC), f32)] + [pltpu.VMEM((PB, TC), bf16)] * 4
        + [pltpu.VMEM((CR, TC), bf16)] * 2,
        compiler_params=pltpu.CompilerParams(vmem_limit_bytes=48 * MB),
    )(at, window, panel, got, trail, child, *factors)


def flip(x, axis, bit, size):
    return lax.ppermute(x, axis, [(i, i ^ bit) for i in range(size)])


def window_pairs(w, parity):
    pairs = []
    for c in range(16):
        if (c + 2) % 3 == w:
            for r in range(8):
                pairs.append((((c + 2) // 3) * 16 + 2 * r + parity, r * 16 + c))
    return pairs


def on_device(front_panel, front_trail, child_panel, child_trail, child_map, child_count):
    row = lax.axis_index("row")
    col = lax.axis_index("col")
    at = jnp.stack([row, col]).astype(jnp.int32)

    own, send = panel_parts(child_count, child_map, front_panel.T, child_panel.transpose(0, 2, 1))
    got = flip(send, "row", 4, 8)
    own0 = lax.ppermute(own[:, :PB], "row", [(0, 4)])
    trail = trail_own(child_count, child_map, front_trail, child_trail)
    panel_t = own + got[:PC]

    diag = jnp.where(row == 4, own0 + send[:PC, :PB], panel_t[:, :PB])
    odd = jnp.bitwise_and(row, 1)
    lo, hi = diag[:, :512], diag[:, 512:]
    pieces = [
        lax.ppermute(hi, "row", [(0, 1), (4, 5)]),
        lax.ppermute(lo, "row", [(0, 2), (4, 6)]),
        lax.ppermute(hi, "row", [(0, 3), (4, 7)]),
    ]
    half = pieces[0] + pieces[1] + pieces[2] + jnp.where(row % 4 == 0, lo, 0.0)
    x4 = jnp.stack([half] + [flip(half, "col", b, 16) for b in (1, 2, 3)])
    y4 = jnp.stack([x4] + [flip(x4, "col", b, 16) for b in (4, 8, 12)]).reshape(16, PC, 512)
    other = flip(y4, "row", 1, 8)
    low = jnp.where(odd == 0, y4, other)
    high = jnp.where(odd == 0, other, y4)
    d_pieces = jnp.concatenate([low, high], axis=2)

    panel_full = lax.all_gather(panel_t, "col", axis=0, tiled=True)

    parts = []
    for parity in range(2):
        got_w = [
            lax.ppermute(panel_t[:, 512 * w:512 * (w + 1)], ("row", "col"), window_pairs(w, parity))
            for w in range(3)
        ]
        parts.append(got_w[0] + got_w[1] + got_w[2])
    win = jnp.concatenate(parts, axis=0)
    z4 = jnp.stack([win] + [flip(win, "row", b, 8) for b in (2, 4, 6)])
    zo = flip(z4, "row", 1, 8)
    window = jnp.stack([z4, zo], axis=1).reshape(8, B, TC)

    child1 = flip(child_trail[1], "row", 4, 8)
    factors = cholesky(at, d_pieces)
    factor_t, schur = finish(at, window, panel_full, got, trail, child1, factors)
    return factor_t.T, schur


def solution(mesh):
    in_specs = (
        P("row", "col"),
        P("row", "col"),
        P(None, "row", "col"),
        P(None, "row", "col"),
        P(None, "row"),
        P(None, "row"),
    )
    out_specs = (P("row", "col"), P("row", "col"))
    return jax.shard_map(
        on_device, mesh=mesh, in_specs=in_specs, out_specs=out_specs, check_vma=False
    )
```

```python
import jax
import jax.numpy as jnp
from jax import lax
from jax.experimental import pallas as pl
from jax.experimental.pallas import tpu as pltpu
from jax.sharding import PartitionSpec as P

f32 = jnp.float32
bf16 = jnp.bfloat16

F = 12288
PB = 1024
CR = 1024
FR = 1536
TC = 512
PC = 64
B = 128
NB = PB // B
Q = 256
HF = 512
MB = 1 << 20

NATURAL = (((1,), (0,)), ((), ()))
LHS_T = (((0,), (0,)), ((), ()))
RHS_T = (((1,), (1,)), ((), ()))


def split(x):
    hi = x.astype(bf16)
    return hi, (x - hi.astype(f32)).astype(bf16)


def dot1(a, b, dims=NATURAL):
    return lax.dot_general(a, b, dims, preferred_element_type=f32)


def dot3(a, b, dims=NATURAL):
    (ah, al), (bh, bl) = a, b
    return dot1(ah, bh, dims) + (dot1(ah, bl, dims) + dot1(al, bh, dims))


def one_hot(first, rows, target):
    at = first + lax.broadcasted_iota(jnp.int32, (rows, CR), 0)
    return (at == target).astype(f32).astype(bf16)


def live_target(count, map_row):
    k = lax.broadcasted_iota(jnp.int32, (1, CR), 1)
    return jnp.where(k < count, map_row, -1)


def panel_kernel(at_ref, count_ref, map_ref, front_ref, child_ref, own_ref, send_ref, crit_ref):
    for slab in range(2):
        target = live_target(count_ref[0, slab], map_ref[slab:slab + 1, :])
        c = child_ref[slab]
        hi = c.astype(bf16)
        rest = c - hi.astype(f32)
        mid = rest.astype(bf16)
        low = (rest - mid.astype(f32)).astype(bf16)
        parts = jnp.concatenate([hi, mid, low], axis=0)
        for at in range(0, FR, 512):
            moved = dot1(parts, one_hot(at, 512, target), RHS_T)
            moved = moved[:PC] + (moved[PC:2 * PC] + moved[2 * PC:])
            if slab == 0:
                own_ref[:, at:at + 512] = front_ref[:, at:at + 512] + moved
            else:
                send_ref[:PC, at:at + 512] = moved
        if slab == 1:
            send_ref[PC:, :CR] = jnp.broadcast_to(target.astype(f32), (8, CR))
            send_ref[PC:, CR:] = jnp.zeros((8, FR - CR), f32)
    crit_ref[...] = send_ref[:PC, :PB]

    @pl.when(at_ref[0] == 0)
    def _():
        crit_ref[...] = own_ref[:, :PB]


def panel_parts(at, count, child_map, front_t, child_t):
    return pl.pallas_call(
        panel_kernel,
        name="panel_parts",
        out_shape=(
            jax.ShapeDtypeStruct((PC, FR), f32),
            jax.ShapeDtypeStruct((PC + 8, FR), f32),
            jax.ShapeDtypeStruct((PC, PB), f32),
        ),
        in_specs=[pl.BlockSpec(memory_space=pltpu.SMEM)] * 2 + [pl.BlockSpec(memory_space=pltpu.VMEM)] * 3,
        out_specs=(pl.BlockSpec(memory_space=pltpu.VMEM),) * 3,
        compiler_params=pltpu.CompilerParams(vmem_limit_bytes=58 * MB),
    )(at, count, child_map, front_t, child_t)


def trail_kernel(count_ref, map_ref, front_ref, child_ref, out_ref, ch, cl):
    @pl.when(pl.program_id(0) == 0)
    def _():
        ch[...], cl[...] = split(child_ref[...])

    target = live_target(count_ref[0, 0], map_ref[0:1, :])
    g = one_hot(pl.program_id(0) * 512, 512, target)
    out_ref[...] = front_ref[...] + (dot1(g, ch[...]) + dot1(g, cl[...]))


def trail_own(count, child_map, front, child):
    return pl.pallas_call(
        trail_kernel,
        name="trail_own",
        grid=(FR // 512,),
        out_shape=jax.ShapeDtypeStruct((FR, TC), f32),
        in_specs=[
            pl.BlockSpec(memory_space=pltpu.SMEM),
            pl.BlockSpec((2, CR), lambda s: (0, 0)),
            pl.BlockSpec((512, TC), lambda s: (s, 0)),
            pl.BlockSpec((None, CR, TC), lambda s: (0, 0, 0)),
        ],
        out_specs=pl.BlockSpec((512, TC), lambda s: (s, 0)),
        scratch_shapes=[pltpu.VMEM((CR, TC), bf16)] * 2,
        compiler_params=pltpu.CompilerParams(vmem_limit_bytes=58 * MB),
    )(count, child_map, front, child)


def lane(x, at):
    return jnp.broadcast_to(x[:, at:at + 1], (8, B))


def chain(w_ref):
    def rows(r):
        x = jnp.broadcast_to(w_ref[r:r + 1, :], (8, 2 * B))
        return x[:, :B], x[:, B:]

    for q in range(4):
        done = []
        for t in range(4):
            m = 4 * q + t
            p, a = [], []
            for i in range(8):
                x, y = rows(8 * m + i)
                p.append(x)
                a.append(y)

            def apply(u):
                b = [[lane(u[j][0], 8 * m + i) for j in range(8)] for i in range(8)]
                for i in range(8):
                    for j in range(8):
                        p[i] = p[i] - b[i][j] * u[j][0]
                        a[i] = a[i] - b[i][j] * u[j][1]
                return b

            for u in done[:-1]:
                apply(u)
            d = {(i, j): lane(p[i], 8 * m + j) for i in range(8) for j in range(i + 1)}
            if done:
                b = apply(done[-1])
                for i in range(8):
                    for j in range(i + 1):
                        for k in range(8):
                            d[i, j] = d[i, j] - b[i][k] * b[j][k]
            u = []
            for j in range(8):
                r = lax.rsqrt(d[j, j])
                low = {i: d[i, j] * r for i in range(j + 1, 8)}
                for i in range(j + 1, 8):
                    for k in range(j + 1, i + 1):
                        d[i, k] = d[i, k] - low[i] * low[k]
                uj, vj = p[j] * r, a[j] * r
                u.append((uj, vj))
                for i in range(j + 1, 8):
                    p[i] = p[i] - low[i] * uj
                    a[i] = a[i] - low[i] * vj
            sub = lax.broadcasted_iota(jnp.int32, (8, B), 0)
            cu, cv = u[0]
            for j in range(1, 8):
                cu = jnp.where(sub == j, u[j][0], cu)
                cv = jnp.where(sub == j, u[j][1], cv)
            w_ref[8 * m:8 * m + 8, :B] = cu
            w_ref[8 * m:8 * m + 8, B:] = cv
            done.append(u)
        if q < 3:
            um = w_ref[32 * q:32 * q + 32, :]
            ut = um[:, :B].T[32 * (q + 1):, :]
            w_ref[32 * (q + 1):, :] = w_ref[32 * (q + 1):, :] - dot3(split(ut), split(um))


def factor_blocks(rows, width, s_ref, w_ref, v_ref, uh, ul, lh, ll, ih, il):
    r = lax.broadcasted_iota(jnp.int32, (B, B), 0)
    c = lax.broadcasted_iota(jnp.int32, (B, B), 1)
    eye = (r == c).astype(f32)

    def step(k, _):
        for kk in range(rows // B):
            @pl.when(k == kk)
            def _():
                here = slice(kk * B, (kk + 1) * B)
                if kk:
                    left = (lh[here, :kk * B], ll[here, :kk * B])
                    right = (uh[:kk * B, kk * B:], ul[:kk * B, kk * B:])
                    s_ref[here, kk * B:] = s_ref[here, kk * B:] - dot3(left, right)
                w_ref[:, :B] = s_ref[here, here]

        w_ref[:, B:] = eye
        chain(w_ref)
        v = w_ref[:, B:]
        v_ref[k % 2] = v
        vs = split(v)
        for kk in range(rows // B):
            @pl.when(k == kk)
            def _():
                here = slice(kk * B, (kk + 1) * B)
                rest = slice((kk + 1) * B, width)
                dh, dl = split(jnp.where(r <= c, w_ref[:, :B], 0.0))
                lh[here, here] = dh.T
                ll[here, here] = dl.T
                if kk < width // B - 1:
                    rh, rl = split(dot3(vs, split(s_ref[here, rest])))
                    uh[here, rest] = rh
                    ul[here, rest] = rl
                    lh[rest, here] = rh.T
                    ll[rest, here] = rl.T
                if kk < rows // B - 1:
                    lh[here, (kk + 1) * B:rows] = jnp.zeros((B, rows - (kk + 1) * B), bf16)
                    ll[here, (kk + 1) * B:rows] = jnp.zeros((B, rows - (kk + 1) * B), bf16)
                half = kk % 2
                at = half * B
                ih[kk // 2, at:at + B, at:at + B] = vs[0]
                il[kk // 2, at:at + B, at:at + B] = vs[1]
                if half:
                    before = slice((kk - 1) * B, kk * B)
                    first = split(v_ref[0])
                    cross = split(dot3((lh[here, before], ll[here, before]), first))
                    th, tl = split(-dot3(vs, cross))
                    ih[kk // 2, B:, :B] = th
                    il[kk // 2, B:, :B] = tl
                    ih[kk // 2, :B, B:] = jnp.zeros((B, B), bf16)
                    il[kk // 2, :B, B:] = jnp.zeros((B, B), bf16)
        return 0

    lax.fori_loop(0, rows // B, step, 0)


def chol_head_kernel(at_ref, *refs):
    pieces = refs[:8]
    lh, ll, ih, il, next_ref, uh, ul, s_ref, w_ref, v_ref = refs[8:]
    row = at_ref[0]
    col = at_ref[1]
    for par in range(2):
        @pl.when(row % 2 == par)
        def _():
            for k in range(16):
                here = pl.ds(pl.multiple_of(jnp.bitwise_xor(col, k) * PC, PC), PC)
                s_ref[here, 512 * par:512 * (par + 1)] = pieces[k // 4][k % 4]
                s_ref[here, 512 * (1 - par):512 * (2 - par)] = pieces[4 + k // 4][k % 4]
    for i in range(NB):
        for j in range(i, NB):
            up = s_ref[i * B:(i + 1) * B, j * B:(j + 1) * B]
            dn = s_ref[j * B:(j + 1) * B, i * B:(i + 1) * B]
            s_ref[i * B:(i + 1) * B, j * B:(j + 1) * B] = 0.5 * (up + dn.T)
    factor_blocks(HF, PB, s_ref, w_ref, v_ref, uh, ul, lh, ll, ih, il)
    left = (lh[HF:, :], ll[HF:, :])
    next_ref[...] = s_ref[HF:, HF:] - dot3(left, (uh[:, HF:], ul[:, HF:]))


def chol_tail_kernel(s_in, lh, ll, ih, il, uh, ul, s_ref, w_ref, v_ref):
    s_ref[...] = s_in[...]
    factor_blocks(HF, HF, s_ref, w_ref, v_ref, uh, ul, lh, ll, ih, il)


def chol_call(kernel, name, width, extra_out, args):
    part = jax.ShapeDtypeStruct((width, HF), bf16)
    inv = jax.ShapeDtypeStruct((HF // Q, Q, Q), bf16)
    vmem = pl.BlockSpec(memory_space=pltpu.VMEM)
    return pl.pallas_call(
        kernel,
        name=name,
        out_shape=(part, part, inv, inv) + extra_out,
        in_specs=[pl.BlockSpec(memory_space=pltpu.SMEM) if a.dtype == jnp.int32 else vmem for a in args],
        out_specs=(vmem,) * (4 + len(extra_out)),
        scratch_shapes=[
            pltpu.VMEM((HF, width), bf16),
            pltpu.VMEM((HF, width), bf16),
            pltpu.VMEM((width, width), f32),
            pltpu.VMEM((B, 2 * B), f32),
            pltpu.VMEM((2, B, B), f32),
        ],
        compiler_params=pltpu.CompilerParams(vmem_limit_bytes=58 * MB),
        cost_estimate=pl.CostEstimate(flops=25_000_000_000, transcendentals=0, bytes_accessed=8 * MB),
    )(*args)


def chol_head(at, pieces):
    nxt = jax.ShapeDtypeStruct((HF, HF), f32)
    return chol_call(chol_head_kernel, "chol_head", PB, (nxt,), [at, *pieces])


def chol_tail(nxt):
    return chol_call(chol_tail_kernel, "chol_tail", HF, (), [nxt])


def finish_kernel(at_ref, w0, w1, w2, w3, pan, got, trail, child_a, child_b,
                  lh1, ll1, ih1, il1, lh2, ll2, ih2, il2,
                  fac_out, out_out,
                  a_ref, p_ref, t_ref, c_ref, g_ref, lh, ll, ih, il, xh, xl, wh, wl, ch, cl,
                  fac_ref, out_ref, sem, pan_sem, trail_sem, out_sem):
    row = at_ref[0]
    col = at_ref[1]
    copy = pltpu.make_async_copy
    lo, hi = pl.ds(0, HF), pl.ds(HF, HF)
    loads = [
        copy(ih1, ih.at[pl.ds(0, 2)], sem.at[0]), copy(il1, il.at[pl.ds(0, 2)], sem.at[1]),
        copy(lh1, lh.at[:, lo], sem.at[2]), copy(ll1, ll.at[:, lo], sem.at[3]),
        copy(ih2, ih.at[pl.ds(2, 2)], sem.at[4]), copy(il2, il.at[pl.ds(2, 2)], sem.at[5]),
        copy(lh2, lh.at[hi, hi], sem.at[6]), copy(ll2, ll.at[hi, hi], sem.at[7]),
    ]
    for k in range(8):
        here = pl.ds(pl.multiple_of(jnp.bitwise_xor(row, k) * B, B), B)
        loads.append(copy((w0, w1, w2, w3)[k // 2].at[k % 2], a_ref.at[here], sem.at[8 + k]))
    late = [
        copy(child_a, c_ref.at[pl.ds(0, CR // 2)], sem.at[16]),
        copy(child_b, c_ref.at[pl.ds(CR // 2, CR // 2)], sem.at[17]),
        copy(got.at[pl.ds(PC, 8)], g_ref, sem.at[18]),
    ]

    def panel_copy(n):
        return copy(pan.at[:, pl.ds(n * 512, 512)], p_ref.at[n], pan_sem.at[n])

    def trail_copy(n):
        return copy(trail.at[pl.ds(n * 512, 512)], t_ref.at[n], trail_sem.at[n])

    def fac_copy(n):
        return copy(fac_ref.at[n], fac_out.at[:, pl.ds(n * 512, 512)], out_sem.at[n])

    def out_copy(n):
        return copy(out_ref.at[n], out_out.at[pl.ds(n * 512, 512)], out_sem.at[3 + n])

    for d in loads:
        d.start()
    panel_copy(0).start()
    for d in late:
        d.start()
    for n in range(3):
        if n:
            panel_copy(n).start()
        trail_copy(n).start()
    for d in loads:
        d.wait()

    def solve(src, yh, yl):
        for k in range(PB // Q):
            here = slice(k * Q, (k + 1) * Q)
            v = src[here, :]
            if k:
                v = v - dot3((lh[here, :k * Q], ll[here, :k * Q]), (yh[:k * Q, :], yl[:k * Q, :]))
            yh[here, :], yl[here, :] = split(dot3((ih[k], il[k]), split(v)))

    solve(a_ref, wh, wl)
    for d in late:
        d.wait()
    ch[...], cl[...] = split(c_ref[...])
    target = g_ref[0:1, :CR].astype(jnp.int32)
    mine = pl.ds(pl.multiple_of(col * PC, PC), PC)

    def block(n, _):
        panel_copy(n).wait()
        own = jnp.logical_and(row == 0, n < 2)

        @pl.when(own)
        def _():
            here = pl.ds(pl.multiple_of(n * 512, 512), 512)
            xh[...] = lh[here, :].T
            xl[...] = ll[here, :].T

        @pl.when(jnp.logical_and(row == 0, n == 0))
        def _():
            xh[HF:, :] = jnp.zeros((HF, 512), bf16)
            xl[HF:, :] = jnp.zeros((HF, 512), bf16)

        @pl.when(jnp.logical_not(own))
        def _():
            solve(p_ref.at[n], xh, xl)

        fac_ref[n] = xh[mine, :].astype(f32) + xl[mine, :].astype(f32)
        fac_copy(n).start()
        g = one_hot(n * 512, 512, target)
        moved = dot1(g, ch[...]) + dot1(g, cl[...])
        prod = dot3((xh[...], xl[...]), (wh[...], wl[...]), LHS_T)
        trail_copy(n).wait()
        out_ref[n] = t_ref[n] + (moved - prod)
        out_copy(n).start()
        return 0

    lax.fori_loop(0, 3, block, 0)
    for n in range(3):
        fac_copy(n).wait()
        out_copy(n).wait()


def finish(at, window, panel, got, trail, child, head, tail):
    hbm = pl.BlockSpec(memory_space=pl.ANY)
    dma = pltpu.SemaphoreType.DMA
    vm = pltpu.VMEM
    return pl.pallas_call(
        finish_kernel,
        name="finish",
        out_shape=(jax.ShapeDtypeStruct((PC, FR), f32), jax.ShapeDtypeStruct((FR, TC), f32)),
        in_specs=[pl.BlockSpec(memory_space=pltpu.SMEM)] + [hbm] * 17,
        out_specs=(hbm, hbm),
        scratch_shapes=[
            vm((PB, TC), f32), vm((3, PB, 512), f32), vm((3, 512, TC), f32), vm((CR, TC), f32),
            vm((8, FR), f32),
            vm((PB, PB), bf16), vm((PB, PB), bf16),
            vm((PB // Q, Q, Q), bf16), vm((PB // Q, Q, Q), bf16),
            vm((PB, 512), bf16), vm((PB, 512), bf16), vm((PB, TC), bf16), vm((PB, TC), bf16),
            vm((CR, TC), bf16), vm((CR, TC), bf16),
            vm((3, PC, 512), f32), vm((3, 512, TC), f32),
            dma((19,)), dma((3,)), dma((3,)), dma((6,)),
        ],
        compiler_params=pltpu.CompilerParams(vmem_limit_bytes=58 * MB),
        cost_estimate=pl.CostEstimate(flops=15_000_000_000, transcendentals=0, bytes_accessed=25 * MB),
    )(at, *window, panel, got, trail, *child, *head, *tail)


def flip(x, axis, bit, size):
    return lax.ppermute(x, axis, [(i, i ^ bit) for i in range(size)])


def window_pairs(step):
    pairs = []
    for c in range(16):
        for parity in range(2):
            if ((c + 2) % 3 + parity) % 3 == step:
                for r in range(8):
                    pairs.append((((c + 2) // 3) * 16 + 2 * r + parity, r * 16 + c))
    return pairs


def on_device(front_panel, front_trail, child_panel, child_trail, child_map, child_count):
    row = lax.axis_index("row")
    col = lax.axis_index("col")
    at = jnp.stack([row, col]).astype(jnp.int32)

    count = child_count.T
    own, send, crit = panel_parts(
        at, count, child_map, front_panel.T, child_panel.transpose(0, 2, 1)
    )
    there = lax.ppermute(crit, "row", [(0, 4), (4, 0)])
    there, send = lax.optimization_barrier((there, send))
    got = flip(send, "row", 4, 8)
    diag = crit + there
    lo, hi = diag[:, :512], diag[:, 512:]
    half = jnp.where(row % 4 == 0, lo, 0.0)
    for k, part in ((1, hi), (2, lo), (3, hi)):
        half = half + lax.ppermute(part, "row", [(0, k), (4, 4 + k)])
    x4 = jnp.stack([half] + [flip(half, "col", b, 16) for b in (1, 2, 3)])
    x4, got, count, child_a = lax.optimization_barrier((x4, got, count, child_trail[1, :CR // 2]))
    child_a = flip(child_a, "row", 4, 8)
    mine = [x4] + [flip(x4, "col", b, 16) for b in (4, 8, 12)]
    other = [flip(x4, "row", 1, 8)]
    panel_t = own + got[:PC]
    trail = trail_own(count, child_map, front_trail, child_trail)
    *mine, panel_t, trail, child_a, child_b = lax.optimization_barrier(
        (*mine, panel_t, trail, child_a, child_trail[1, CR // 2:])
    )
    other += [flip(piece, "row", 1, 8) for piece in mine[1:]]
    panel_full = lax.all_gather(panel_t, "col", axis=0, tiled=True)
    child_b = flip(child_b, "row", 4, 8)

    odd = jnp.bitwise_and(col, 1)
    panes = [panel_t[:, 512 * w:512 * (w + 1)] for w in range(3)]
    steps = [
        lax.ppermute(jnp.where(odd == 0, panes[k], panes[(k + 2) % 3]), ("row", "col"), window_pairs(k))
        for k in range(3)
    ]
    *head, nxt = chol_head(at, mine + other)
    *steps, nxt, child_b = lax.optimization_barrier((*steps, nxt, child_b))
    at_w = (col + 2) % 3
    first = jnp.where(at_w == 0, steps[0], jnp.where(at_w == 1, steps[1], steps[2]))
    second = jnp.where(at_w == 0, steps[1], jnp.where(at_w == 1, steps[2], steps[0]))
    win = jnp.concatenate([first, second], axis=0)
    pair = jnp.stack([win, flip(win, "row", 1, 8)])
    window = [pair] + [flip(pair, "row", b, 8) for b in (2, 4, 6)]
    tail = chol_tail(nxt)

    factor_t, schur = finish(at, window, panel_full, got, trail, [child_a, child_b], head, tail)
    return factor_t.T, schur


def solution(mesh):
    in_specs = (
        P("row", "col"),
        P("row", "col"),
        P(None, "row", "col"),
        P(None, "row", "col"),
        P(None, "row"),
        P(None, "row"),
    )
    out_specs = (P("row", "col"), P("row", "col"))
    return jax.shard_map(
        on_device, mesh=mesh, in_specs=in_specs, out_specs=out_specs, check_vma=False
    )
```

```python
import jax
import jax.numpy as jnp
from jax import lax
from jax.experimental import pallas as pl
from jax.experimental.pallas import tpu as pltpu
from jax.sharding import PartitionSpec as P

f32 = jnp.float32
bf16 = jnp.bfloat16

F = 12288
PB = 1024
CR = 1024
FR = 1536
TC = 512
PC = 64
B = 128
NB = PB // B
Q = 256
HF = 512
EA = 576
MB = 1 << 20

NATURAL = (((1,), (0,)), ((), ()))
LHS_T = (((0,), (0,)), ((), ()))
RHS_T = (((1,), (1,)), ((), ()))


def split(x):
    hi = x.astype(bf16)
    return hi, (x - hi.astype(f32)).astype(bf16)


def dot1(a, b, dims=NATURAL):
    return lax.dot_general(a, b, dims, preferred_element_type=f32)


def dot3(a, b, dims=NATURAL):
    (ah, al), (bh, bl) = a, b
    return dot1(ah, bh, dims) + (dot1(ah, bl, dims) + dot1(al, bh, dims))


def one_hot(first, rows, target):
    at = first + lax.broadcasted_iota(jnp.int32, (rows, CR), 0)
    return (at == target).astype(f32).astype(bf16)


def live_target(count, map_row):
    k = lax.broadcasted_iota(jnp.int32, (1, CR), 1)
    return jnp.where(k < count, map_row, -1)


def panel_kernel(at_ref, count_ref, map_ref, front_ref, child_ref, own_ref, send_ref, crit_ref):
    for slab in range(2):
        target = live_target(count_ref[0, slab], map_ref[slab:slab + 1, :])
        c = child_ref[slab]
        hi = c.astype(bf16)
        rest = c - hi.astype(f32)
        mid = rest.astype(bf16)
        low = (rest - mid.astype(f32)).astype(bf16)
        parts = jnp.concatenate([hi, mid, low], axis=0)
        for at in range(0, FR, 512):
            moved = dot1(parts, one_hot(at, 512, target), RHS_T)
            moved = moved[:PC] + (moved[PC:2 * PC] + moved[2 * PC:])
            if slab == 0:
                own_ref[:, at:at + 512] = front_ref[:, at:at + 512] + moved
            else:
                send_ref[:PC, at:at + 512] = moved
        if slab == 1:
            send_ref[PC:, :CR] = jnp.broadcast_to(target.astype(f32), (8, CR))
            send_ref[PC:, CR:] = jnp.zeros((8, FR - CR), f32)
    crit_ref[...] = send_ref[:PC, :PB]

    @pl.when(at_ref[0] == 0)
    def _():
        crit_ref[...] = own_ref[:, :PB]


def panel_parts(at, count, child_map, front_t, child_t):
    return pl.pallas_call(
        panel_kernel,
        name="panel_parts",
        out_shape=(
            jax.ShapeDtypeStruct((PC, FR), f32),
            jax.ShapeDtypeStruct((PC + 8, FR), f32),
            jax.ShapeDtypeStruct((PC, PB), f32),
        ),
        in_specs=[pl.BlockSpec(memory_space=pltpu.SMEM)] * 2 + [pl.BlockSpec(memory_space=pltpu.VMEM)] * 3,
        out_specs=(pl.BlockSpec(memory_space=pltpu.VMEM),) * 3,
        compiler_params=pltpu.CompilerParams(vmem_limit_bytes=58 * MB),
    )(at, count, child_map, front_t, child_t)


def trail_kernel(count_ref, map_ref, front_ref, child_ref, out_ref, ch, cl):
    @pl.when(pl.program_id(0) == 0)
    def _():
        ch[...], cl[...] = split(child_ref[...])

    target = live_target(count_ref[0, 0], map_ref[0:1, :])
    g = one_hot(pl.program_id(0) * 512, 512, target)
    out_ref[...] = front_ref[...] + (dot1(g, ch[...]) + dot1(g, cl[...]))


def trail_own(count, child_map, front, child):
    return pl.pallas_call(
        trail_kernel,
        name="trail_own",
        grid=(FR // 512,),
        out_shape=jax.ShapeDtypeStruct((FR, TC), f32),
        in_specs=[
            pl.BlockSpec(memory_space=pltpu.SMEM),
            pl.BlockSpec((2, CR), lambda s: (0, 0)),
            pl.BlockSpec((512, TC), lambda s: (s, 0)),
            pl.BlockSpec((None, CR, TC), lambda s: (0, 0, 0)),
        ],
        out_specs=pl.BlockSpec((512, TC), lambda s: (s, 0)),
        scratch_shapes=[pltpu.VMEM((CR, TC), bf16)] * 2,
        compiler_params=pltpu.CompilerParams(vmem_limit_bytes=58 * MB),
    )(count, child_map, front, child)


def lane(x, at):
    return jnp.broadcast_to(x[:, at:at + 1], (8, B))


def chain(w_ref):
    sub = lax.broadcasted_iota(jnp.int32, (8, B), 0)
    for m in range(B // 8):
        here = slice(8 * m, 8 * m + 8)
        p, a = [], []
        for i in range(8):
            x = jnp.broadcast_to(w_ref[8 * m + i:8 * m + i + 1, :], (8, 2 * B))
            p.append(x[:, :B])
            a.append(x[:, B:])
        d = {(i, j): lane(p[i], 8 * m + j) for i in range(8) for j in range(i + 1)}
        near = m + 1 < B // 8
        if near:
            at = slice(8 * m + 8, 8 * m + 16)
            np_, na = w_ref[at, :B], w_ref[at, B:]
            c = [lane(np_, 8 * m + j) for j in range(8)]
        u, v, r, low = [], [], [], {}
        for j in range(8):
            r.append(lax.rsqrt(d[j, j]))
            for i in range(j + 1, 8):
                low[i, j] = d[i, j] * r[j]
            for i in range(j + 1, 8):
                for k in range(j + 1, i + 1):
                    d[i, k] = d[i, k] - low[i, j] * low[k, j]
            u.append(p[j] * r[j])
            v.append(a[j] * r[j])
            for i in range(j + 1, 8):
                p[i] = p[i] - low[i, j] * u[j]
                a[i] = a[i] - low[i, j] * v[j]
            if near:
                cj = c[j] * r[j]
                for i in range(j + 1, 8):
                    c[i] = c[i] - low[i, j] * cj
                np_ = np_ - cj * u[j]
                na = na - cj * v[j]
        if near:
            w_ref[at, :B] = np_
            w_ref[at, B:] = na
        cu, cv = u[0], v[0]
        for j in range(1, 8):
            cu = jnp.where(sub == j, u[j], cu)
            cv = jnp.where(sub == j, v[j], cv)
        w_ref[here, :B] = cu
        w_ref[here, B:] = cv
        if m + 2 < B // 8:
            for n in range(m + 2, B // 8):
                at = slice(8 * n, 8 * n + 8)
                x, y = w_ref[at, :B], w_ref[at, B:]
                c = [lane(x, 8 * m + j) for j in range(8)]
                g, h = u, v
                for j in range(8):
                    c[j] = c[j] * r[j]
                    for i in range(j + 1, 8):
                        c[i] = c[i] - low[i, j] * c[j]
                sx = [c[j] * g[j] for j in range(8)]
                sy = [c[j] * h[j] for j in range(8)]
                while len(sx) > 1:
                    sx = [sx[k] + sx[k + 1] for k in range(0, len(sx), 2)]
                    sy = [sy[k] + sy[k + 1] for k in range(0, len(sy), 2)]
                w_ref[at, :B] = x - sx[0]
                w_ref[at, B:] = y - sy[0]


def factor_blocks(rows, width, s_ref, w_ref, v_ref, uh, ul, lh, ll, ih, il):
    r = lax.broadcasted_iota(jnp.int32, (B, B), 0)
    c = lax.broadcasted_iota(jnp.int32, (B, B), 1)
    eye = (r == c).astype(f32)

    def step(k, _):
        for kk in range(rows // B):
            @pl.when(k == kk)
            def _():
                here = slice(kk * B, (kk + 1) * B)
                if kk:
                    left = (lh[here, :kk * B], ll[here, :kk * B])
                    right = (uh[:kk * B, kk * B:], ul[:kk * B, kk * B:])
                    s_ref[here, kk * B:] = s_ref[here, kk * B:] - dot3(left, right)
                w_ref[:, :B] = s_ref[here, here]

        w_ref[:, B:] = eye
        chain(w_ref)
        v = w_ref[:, B:]
        v_ref[k % 2] = v
        vs = split(v)
        for kk in range(rows // B):
            @pl.when(k == kk)
            def _():
                here = slice(kk * B, (kk + 1) * B)
                rest = slice((kk + 1) * B, width)
                dh, dl = split(jnp.where(r <= c, w_ref[:, :B], 0.0))
                lh[here, here] = dh.T
                ll[here, here] = dl.T
                if kk < width // B - 1:
                    rh, rl = split(dot3(vs, split(s_ref[here, rest])))
                    uh[here, rest] = rh
                    ul[here, rest] = rl
                    lh[rest, here] = rh.T
                    ll[rest, here] = rl.T
                if kk < rows // B - 1:
                    lh[here, (kk + 1) * B:rows] = jnp.zeros((B, rows - (kk + 1) * B), bf16)
                    ll[here, (kk + 1) * B:rows] = jnp.zeros((B, rows - (kk + 1) * B), bf16)
                half = kk % 2
                at = half * B
                ih[kk // 2, at:at + B, at:at + B] = vs[0]
                il[kk // 2, at:at + B, at:at + B] = vs[1]
                if half:
                    before = slice((kk - 1) * B, kk * B)
                    first = split(v_ref[0])
                    cross = split(dot3((lh[here, before], ll[here, before]), first))
                    th, tl = split(-dot3(vs, cross))
                    ih[kk // 2, B:, :B] = th
                    il[kk // 2, B:, :B] = tl
                    ih[kk // 2, :B, B:] = jnp.zeros((B, B), bf16)
                    il[kk // 2, :B, B:] = jnp.zeros((B, B), bf16)
        return 0

    lax.fori_loop(0, rows // B, step, 0)


def chol_head_kernel(at_ref, *refs):
    pieces = refs[:8]
    lh, ll, ih, il, next_ref, uh, ul, s_ref, w_ref, v_ref = refs[8:]
    row = at_ref[0]
    col = at_ref[1]
    for par in range(2):
        @pl.when(row % 2 == par)
        def _():
            for k in range(16):
                here = pl.ds(pl.multiple_of(jnp.bitwise_xor(col, k) * PC, PC), PC)
                s_ref[here, 512 * par:512 * (par + 1)] = pieces[k // 4][k % 4]
                s_ref[here, 512 * (1 - par):512 * (2 - par)] = pieces[4 + k // 4][k % 4]
    for i in range(NB):
        for j in range(i, NB):
            up = s_ref[i * B:(i + 1) * B, j * B:(j + 1) * B]
            dn = s_ref[j * B:(j + 1) * B, i * B:(i + 1) * B]
            s_ref[i * B:(i + 1) * B, j * B:(j + 1) * B] = 0.5 * (up + dn.T)
    factor_blocks(HF, PB, s_ref, w_ref, v_ref, uh, ul, lh, ll, ih, il)
    left = (lh[HF:, :], ll[HF:, :])
    next_ref[...] = s_ref[HF:, HF:] - dot3(left, (uh[:, HF:], ul[:, HF:]))


def chol_tail_kernel(s_in, lh, ll, ih, il, uh, ul, s_ref, w_ref, v_ref):
    s_ref[...] = s_in[...]
    factor_blocks(HF, HF, s_ref, w_ref, v_ref, uh, ul, lh, ll, ih, il)


def chol_call(kernel, name, width, extra_out, args):
    part = jax.ShapeDtypeStruct((width, HF), bf16)
    inv = jax.ShapeDtypeStruct((HF // Q, Q, Q), bf16)
    vmem = pl.BlockSpec(memory_space=pltpu.VMEM)
    return pl.pallas_call(
        kernel,
        name=name,
        out_shape=(part, part, inv, inv) + extra_out,
        in_specs=[pl.BlockSpec(memory_space=pltpu.SMEM) if a.dtype == jnp.int32 else vmem for a in args],
        out_specs=(vmem,) * (4 + len(extra_out)),
        scratch_shapes=[
            pltpu.VMEM((HF, width), bf16),
            pltpu.VMEM((HF, width), bf16),
            pltpu.VMEM((width, width), f32),
            pltpu.VMEM((B, 2 * B), f32),
            pltpu.VMEM((2, B, B), f32),
        ],
        compiler_params=pltpu.CompilerParams(vmem_limit_bytes=58 * MB),
        cost_estimate=pl.CostEstimate(flops=25_000_000_000, transcendentals=0, bytes_accessed=8 * MB),
    )(*args)


def chol_head(at, pieces):
    nxt = jax.ShapeDtypeStruct((HF, HF), f32)
    return chol_call(chol_head_kernel, "chol_head", PB, (nxt,), [at, *pieces])


def chol_tail(nxt):
    return chol_call(chol_tail_kernel, "chol_tail", HF, (), [nxt])


def finish_kernel(at_ref, w0, w1, w2, w3, pan, got, trail, child_a, child_b,
                  lh1, ll1, ih1, il1, lh2, ll2, ih2, il2,
                  fac_out, out_out,
                  a_ref, p_ref, t_ref, c_ref, g_ref, lh, ll, ih, il, xh, xl, wh, wl, ch, cl,
                  fac_ref, out_ref, sem, pan_sem, trail_sem, out_sem):
    row = at_ref[0]
    col = at_ref[1]
    copy = pltpu.make_async_copy
    lo, hi = pl.ds(0, HF), pl.ds(HF, HF)
    factors = [
        copy(ih1, ih.at[pl.ds(0, 2)], sem.at[0]), copy(il1, il.at[pl.ds(0, 2)], sem.at[1]),
        copy(lh1, lh.at[:, lo], sem.at[2]), copy(ll1, ll.at[:, lo], sem.at[3]),
        copy(ih2, ih.at[pl.ds(2, 2)], sem.at[4]), copy(il2, il.at[pl.ds(2, 2)], sem.at[5]),
        copy(lh2, lh.at[hi, hi], sem.at[6]), copy(ll2, ll.at[hi, hi], sem.at[7]),
    ]
    window = []
    for k in range(8):
        here = pl.ds(pl.multiple_of(jnp.bitwise_xor(row, k) * B, B), B)
        window.append(copy((w0, w1, w2, w3)[k // 2].at[k % 2], a_ref.at[here], sem.at[8 + k]))
    late = [
        copy(child_a, c_ref.at[pl.ds(0, EA)], sem.at[16]),
        copy(child_b, c_ref.at[pl.ds(EA, CR - EA)], sem.at[17]),
        copy(got.at[pl.ds(PC, 8)], g_ref, sem.at[18]),
    ]

    def panel_copy(n):
        return copy(pan.at[:, pl.ds(n * 512, 512)], p_ref.at[n], pan_sem.at[n])

    def trail_copy(n):
        return copy(trail.at[pl.ds(n * 512, 512)], t_ref.at[n], trail_sem.at[n])

    def fac_copy(n):
        return copy(fac_ref.at[n], fac_out.at[:, pl.ds(n * 512, 512)], out_sem.at[n])

    def out_copy(n):
        return copy(out_ref.at[n], out_out.at[pl.ds(n * 512, 512)], out_sem.at[3 + n])

    for d in factors[:2] + window + factors[2:]:
        d.start()
    panel_copy(0).start()
    for d in late:
        d.start()
    for n in range(3):
        if n:
            panel_copy(n).start()
        trail_copy(n).start()

    def solve(src, yh, yl, needs=((),) * 4):
        for k in range(PB // Q):
            for d in needs[k]:
                d.wait()
            here = slice(k * Q, (k + 1) * Q)
            v = src[here, :]
            if k:
                v = v - dot3((lh[here, :k * Q], ll[here, :k * Q]), (yh[:k * Q, :], yl[:k * Q, :]))
            yh[here, :], yl[here, :] = split(dot3((ih[k], il[k]), split(v)))

    solve(a_ref, wh, wl, (factors[:2] + window, factors[2:4], factors[4:6], factors[6:]))
    for d in late:
        d.wait()
    ch[...], cl[...] = split(c_ref[...])
    target = g_ref[0:1, :CR].astype(jnp.int32)
    mine = pl.ds(pl.multiple_of(col * PC, PC), PC)

    def block(n, _):
        panel_copy(n).wait()
        own = jnp.logical_and(row == 0, n < 2)

        @pl.when(own)
        def _():
            here = pl.ds(pl.multiple_of(n * 512, 512), 512)
            xh[...] = lh[here, :].T
            xl[...] = ll[here, :].T

        @pl.when(jnp.logical_and(row == 0, n == 0))
        def _():
            xh[HF:, :] = jnp.zeros((HF, 512), bf16)
            xl[HF:, :] = jnp.zeros((HF, 512), bf16)

        @pl.when(jnp.logical_not(own))
        def _():
            solve(p_ref.at[n], xh, xl)

        fac_ref[n] = xh[mine, :].astype(f32) + xl[mine, :].astype(f32)
        fac_copy(n).start()
        g = one_hot(n * 512, 512, target)
        moved = dot1(g, ch[...]) + dot1(g, cl[...])
        prod = dot3((xh[...], xl[...]), (wh[...], wl[...]), LHS_T)
        trail_copy(n).wait()
        out_ref[n] = t_ref[n] + (moved - prod)
        out_copy(n).start()
        return 0

    lax.fori_loop(0, 3, block, 0)
    for n in range(3):
        fac_copy(n).wait()
        out_copy(n).wait()


def finish(at, window, panel, got, trail, child, head, tail):
    hbm = pl.BlockSpec(memory_space=pl.ANY)
    dma = pltpu.SemaphoreType.DMA
    vm = pltpu.VMEM
    return pl.pallas_call(
        finish_kernel,
        name="finish",
        out_shape=(jax.ShapeDtypeStruct((PC, FR), f32), jax.ShapeDtypeStruct((FR, TC), f32)),
        in_specs=[pl.BlockSpec(memory_space=pltpu.SMEM)] + [hbm] * 17,
        out_specs=(hbm, hbm),
        scratch_shapes=[
            vm((PB, TC), f32), vm((3, PB, 512), f32), vm((3, 512, TC), f32), vm((CR, TC), f32),
            vm((8, FR), f32),
            vm((PB, PB), bf16), vm((PB, PB), bf16),
            vm((PB // Q, Q, Q), bf16), vm((PB // Q, Q, Q), bf16),
            vm((PB, 512), bf16), vm((PB, 512), bf16), vm((PB, TC), bf16), vm((PB, TC), bf16),
            vm((CR, TC), bf16), vm((CR, TC), bf16),
            vm((3, PC, 512), f32), vm((3, 512, TC), f32),
            dma((19,)), dma((3,)), dma((3,)), dma((6,)),
        ],
        compiler_params=pltpu.CompilerParams(vmem_limit_bytes=58 * MB),
        cost_estimate=pl.CostEstimate(flops=15_000_000_000, transcendentals=0, bytes_accessed=25 * MB),
    )(at, *window, panel, got, trail, *child, *head, *tail)


def flip(x, axis, bit, size):
    return lax.ppermute(x, axis, [(i, i ^ bit) for i in range(size)])


def window_pairs(step):
    pairs = []
    for c in range(16):
        for parity in range(2):
            if ((c + 2) % 3 + parity) % 3 == step:
                for r in range(8):
                    pairs.append((((c + 2) // 3) * 16 + 2 * r + parity, r * 16 + c))
    return pairs


def on_device(front_panel, front_trail, child_panel, child_trail, child_map, child_count):
    row = lax.axis_index("row")
    col = lax.axis_index("col")
    at = jnp.stack([row, col]).astype(jnp.int32)

    count = child_count.T
    own, send, crit = panel_parts(
        at, count, child_map, front_panel.T, child_panel.transpose(0, 2, 1)
    )
    there = lax.ppermute(crit, "row", [(0, 4), (4, 0)])
    there, send = lax.optimization_barrier((there, send))
    got = flip(send, "row", 4, 8)
    diag = crit + there
    lo, hi = diag[:, :512], diag[:, 512:]
    half = jnp.where(row % 4 == 0, lo, 0.0)
    for k, part in ((1, hi), (2, lo), (3, hi)):
        half = half + lax.ppermute(part, "row", [(0, k), (4, 4 + k)])
    x4 = jnp.stack([half] + [flip(half, "col", b, 16) for b in (1, 2, 3)])
    x4, got, count, child_a = lax.optimization_barrier((x4, got, count, child_trail[1, :EA]))
    child_a = flip(child_a, "row", 4, 8)
    mine = [x4] + [flip(x4, "col", b, 16) for b in (4, 8, 12)]
    panel_t = own + got[:PC]
    odd = jnp.bitwise_and(col, 1)
    panes = [panel_t[:, 512 * w:512 * (w + 1)] for w in range(3)]
    picks = [jnp.where(odd == 0, panes[k], panes[(k + 2) % 3]) for k in range(3)]
    trail = trail_own(count, child_map, front_trail, child_trail)
    *mine, panel_t, trail, child_a, child_b, p0, p1, p2 = lax.optimization_barrier(
        (*mine, panel_t, trail, child_a, child_trail[1, EA:], *picks)
    )
    panel_full = lax.all_gather(panel_t, "col", axis=0, tiled=True)
    other = [flip(piece, "row", 1, 8) for piece in mine]
    steps = [lax.ppermute(p, ("row", "col"), window_pairs(k)) for k, p in enumerate((p0, p1, p2))]
    child_b = flip(child_b, "row", 4, 8)

    *head, nxt = chol_head(at, mine + other)
    *steps, nxt, child_b = lax.optimization_barrier((*steps, nxt, child_b))
    at_w = (col + 2) % 3
    first = jnp.where(at_w == 0, steps[0], jnp.where(at_w == 1, steps[1], steps[2]))
    second = jnp.where(at_w == 0, steps[1], jnp.where(at_w == 1, steps[2], steps[0]))
    win = jnp.concatenate([first, second], axis=0)
    pair = jnp.stack([win, flip(win, "row", 1, 8)])
    window = [pair] + [flip(pair, "row", b, 8) for b in (2, 4, 6)]
    tail = chol_tail(nxt)

    factor_t, schur = finish(at, window, panel_full, got, trail, [child_a, child_b], head, tail)
    return factor_t.T, schur


def solution(mesh):
    in_specs = (
        P("row", "col"),
        P("row", "col"),
        P(None, "row", "col"),
        P(None, "row", "col"),
        P(None, "row"),
        P(None, "row"),
    )
    out_specs = (P("row", "col"), P("row", "col"))
    return jax.shard_map(
        on_device, mesh=mesh, in_specs=in_specs, out_specs=out_specs, check_vma=False
    )
```

```python
import jax
import jax.numpy as jnp
from jax import lax
from jax.experimental import pallas as pl
from jax.experimental.pallas import tpu as pltpu
from jax.sharding import PartitionSpec as P

f32 = jnp.float32
bf16 = jnp.bfloat16

F = 12288
PB = 1024
CR = 1024
FR = 1536
TC = 512
PC = 64
B = 128
NB = PB // B
Q = 256
HF = 512
EA = 544
MB = 1 << 20

NATURAL = (((1,), (0,)), ((), ()))
LHS_T = (((0,), (0,)), ((), ()))
RHS_T = (((1,), (1,)), ((), ()))


def split(x):
    hi = x.astype(bf16)
    return hi, (x - hi.astype(f32)).astype(bf16)


def dot1(a, b, dims=NATURAL):
    return lax.dot_general(a, b, dims, preferred_element_type=f32)


def dot3(a, b, dims=NATURAL):
    (ah, al), (bh, bl) = a, b
    return dot1(ah, bh, dims) + (dot1(ah, bl, dims) + dot1(al, bh, dims))


def one_hot(first, rows, target):
    at = first + lax.broadcasted_iota(jnp.int32, (rows, CR), 0)
    return (at == target).astype(f32).astype(bf16)


def live_target(count, map_row):
    k = lax.broadcasted_iota(jnp.int32, (1, CR), 1)
    return jnp.where(k < count, map_row, -1)


def panel_kernel(at_ref, count_ref, map_ref, front_ref, child_ref, own_ref, send_ref, crit_ref):
    for slab in range(2):
        target = live_target(count_ref[0, slab], map_ref[slab:slab + 1, :])
        c = child_ref[slab]
        hi = c.astype(bf16)
        rest = c - hi.astype(f32)
        mid = rest.astype(bf16)
        low = (rest - mid.astype(f32)).astype(bf16)
        parts = jnp.concatenate([hi, mid, low], axis=0)
        for at in range(0, FR, 512):
            moved = dot1(parts, one_hot(at, 512, target), RHS_T)
            moved = moved[:PC] + (moved[PC:2 * PC] + moved[2 * PC:])
            if slab == 0:
                own_ref[:, at:at + 512] = front_ref[:, at:at + 512] + moved
            else:
                send_ref[:PC, at:at + 512] = moved
        if slab == 1:
            send_ref[PC:, :CR] = jnp.broadcast_to(target.astype(f32), (8, CR))
            send_ref[PC:, CR:] = jnp.zeros((8, FR - CR), f32)
    crit_ref[...] = send_ref[:PC, :PB]

    @pl.when(at_ref[0] == 0)
    def _():
        crit_ref[...] = own_ref[:, :PB]


def panel_parts(at, count, child_map, front_t, child_t):
    return pl.pallas_call(
        panel_kernel,
        name="panel_parts",
        out_shape=(
            jax.ShapeDtypeStruct((PC, FR), f32),
            jax.ShapeDtypeStruct((PC + 8, FR), f32),
            jax.ShapeDtypeStruct((PC, PB), f32),
        ),
        in_specs=[pl.BlockSpec(memory_space=pltpu.SMEM)] * 2 + [pl.BlockSpec(memory_space=pltpu.VMEM)] * 3,
        out_specs=(pl.BlockSpec(memory_space=pltpu.VMEM),) * 3,
        compiler_params=pltpu.CompilerParams(vmem_limit_bytes=58 * MB),
    )(at, count, child_map, front_t, child_t)


def trail_kernel(count_ref, map_ref, front_ref, child_ref, out_ref, ch, cl):
    @pl.when(pl.program_id(0) == 0)
    def _():
        ch[...], cl[...] = split(child_ref[...])

    target = live_target(count_ref[0, 0], map_ref[0:1, :])
    g = one_hot(pl.program_id(0) * 512, 512, target)
    out_ref[...] = front_ref[...] + (dot1(g, ch[...]) + dot1(g, cl[...]))


def trail_own(count, child_map, front, child):
    return pl.pallas_call(
        trail_kernel,
        name="trail_own",
        grid=(FR // 512,),
        out_shape=jax.ShapeDtypeStruct((FR, TC), f32),
        in_specs=[
            pl.BlockSpec(memory_space=pltpu.SMEM),
            pl.BlockSpec((2, CR), lambda s: (0, 0)),
            pl.BlockSpec((512, TC), lambda s: (s, 0)),
            pl.BlockSpec((None, CR, TC), lambda s: (0, 0, 0)),
        ],
        out_specs=pl.BlockSpec((512, TC), lambda s: (s, 0)),
        scratch_shapes=[pltpu.VMEM((CR, TC), bf16)] * 2,
        compiler_params=pltpu.CompilerParams(vmem_limit_bytes=58 * MB),
    )(count, child_map, front, child)


def trail_got_kernel(got_ref, trail_ref, a_ref, b_ref, out_ref, ch, cl):
    @pl.when(pl.program_id(0) == 0)
    def _():
        ch[:EA, :], cl[:EA, :] = split(a_ref[...])
        ch[EA:, :], cl[EA:, :] = split(b_ref[...])

    target = got_ref[0:1, :CR].astype(jnp.int32)
    g = one_hot(pl.program_id(0) * 512, 512, target)
    out_ref[...] = trail_ref[...] + (dot1(g, ch[...]) + dot1(g, cl[...]))


def trail_got(got, trail, child_a, child_b):
    return pl.pallas_call(
        trail_got_kernel,
        name="trail_got",
        grid=(FR // 512,),
        out_shape=jax.ShapeDtypeStruct((FR, TC), f32),
        in_specs=[
            pl.BlockSpec((8, FR), lambda s: (PC // 8, 0)),
            pl.BlockSpec((512, TC), lambda s: (s, 0)),
            pl.BlockSpec((EA, TC), lambda s: (0, 0)),
            pl.BlockSpec((CR - EA, TC), lambda s: (0, 0)),
        ],
        out_specs=pl.BlockSpec((512, TC), lambda s: (s, 0)),
        scratch_shapes=[pltpu.VMEM((CR, TC), bf16)] * 2,
        compiler_params=pltpu.CompilerParams(vmem_limit_bytes=58 * MB),
    )(got, trail, child_a, child_b)


def lane(x, at):
    return jnp.broadcast_to(x[:, at:at + 1], (8, B))


def chain(w_ref):
    sub = lax.broadcasted_iota(jnp.int32, (8, B), 0)
    for m in range(B // 8):
        here = slice(8 * m, 8 * m + 8)
        p, a = [], []
        for i in range(8):
            x = jnp.broadcast_to(w_ref[8 * m + i:8 * m + i + 1, :], (8, 2 * B))
            p.append(x[:, :B])
            a.append(x[:, B:])
        d = {(i, j): lane(p[i], 8 * m + j) for i in range(8) for j in range(i + 1)}
        near = m + 1 < B // 8
        if near:
            at = slice(8 * m + 8, 8 * m + 16)
            np_, na = w_ref[at, :B], w_ref[at, B:]
            c = [lane(np_, 8 * m + j) for j in range(8)]
        u, v, r, low = [], [], [], {}
        for j in range(8):
            r.append(lax.rsqrt(d[j, j]))
            for i in range(j + 1, 8):
                low[i, j] = d[i, j] * r[j]
            for i in range(j + 1, 8):
                for k in range(j + 1, i + 1):
                    d[i, k] = d[i, k] - low[i, j] * low[k, j]
            u.append(p[j] * r[j])
            v.append(a[j] * r[j])
            for i in range(j + 1, 8):
                p[i] = p[i] - low[i, j] * u[j]
                a[i] = a[i] - low[i, j] * v[j]
            if near:
                cj = c[j] * r[j]
                for i in range(j + 1, 8):
                    c[i] = c[i] - low[i, j] * cj
                np_ = np_ - cj * u[j]
                na = na - cj * v[j]
        if near:
            w_ref[at, :B] = np_
            w_ref[at, B:] = na
        cu, cv = u[0], v[0]
        for j in range(1, 8):
            cu = jnp.where(sub == j, u[j], cu)
            cv = jnp.where(sub == j, v[j], cv)
        w_ref[here, :B] = cu
        w_ref[here, B:] = cv
        if m + 2 < B // 8:
            for n in range(m + 2, B // 8):
                at = slice(8 * n, 8 * n + 8)
                x, y = w_ref[at, :B], w_ref[at, B:]
                c = [lane(x, 8 * m + j) for j in range(8)]
                g, h = u, v
                for j in range(8):
                    c[j] = c[j] * r[j]
                    for i in range(j + 1, 8):
                        c[i] = c[i] - low[i, j] * c[j]
                sx = [c[j] * g[j] for j in range(8)]
                sy = [c[j] * h[j] for j in range(8)]
                while len(sx) > 1:
                    sx = [sx[k] + sx[k + 1] for k in range(0, len(sx), 2)]
                    sy = [sy[k] + sy[k + 1] for k in range(0, len(sy), 2)]
                w_ref[at, :B] = x - sx[0]
                w_ref[at, B:] = y - sy[0]


def factor_blocks(rows, width, s_ref, w_ref, v_ref, uh, ul, lh, ll, ih, il):
    r = lax.broadcasted_iota(jnp.int32, (B, B), 0)
    c = lax.broadcasted_iota(jnp.int32, (B, B), 1)
    eye = (r == c).astype(f32)

    def step(k, _):
        for kk in range(rows // B):
            @pl.when(k == kk)
            def _():
                here = slice(kk * B, (kk + 1) * B)
                if kk:
                    left = (lh[here, :kk * B], ll[here, :kk * B])
                    right = (uh[:kk * B, kk * B:], ul[:kk * B, kk * B:])
                    s_ref[here, kk * B:] = s_ref[here, kk * B:] - dot3(left, right)
                w_ref[:, :B] = s_ref[here, here]

        w_ref[:, B:] = eye
        chain(w_ref)
        v = w_ref[:, B:]
        v_ref[k % 2] = v
        vs = split(v)
        for kk in range(rows // B):
            @pl.when(k == kk)
            def _():
                here = slice(kk * B, (kk + 1) * B)
                rest = slice((kk + 1) * B, width)
                dh, dl = split(jnp.where(r <= c, w_ref[:, :B], 0.0))
                lh[here, here] = dh.T
                ll[here, here] = dl.T
                if kk < width // B - 1:
                    rh, rl = split(dot3(vs, split(s_ref[here, rest])))
                    uh[here, rest] = rh
                    ul[here, rest] = rl
                    lh[rest, here] = rh.T
                    ll[rest, here] = rl.T
                if kk < rows // B - 1:
                    lh[here, (kk + 1) * B:rows] = jnp.zeros((B, rows - (kk + 1) * B), bf16)
                    ll[here, (kk + 1) * B:rows] = jnp.zeros((B, rows - (kk + 1) * B), bf16)
                half = kk % 2
                at = half * B
                ih[kk // 2, at:at + B, at:at + B] = vs[0]
                il[kk // 2, at:at + B, at:at + B] = vs[1]
                if half:
                    before = slice((kk - 1) * B, kk * B)
                    first = split(v_ref[0])
                    cross = split(dot3((lh[here, before], ll[here, before]), first))
                    th, tl = split(-dot3(vs, cross))
                    ih[kk // 2, B:, :B] = th
                    il[kk // 2, B:, :B] = tl
                    ih[kk // 2, :B, B:] = jnp.zeros((B, B), bf16)
                    il[kk // 2, :B, B:] = jnp.zeros((B, B), bf16)
        return 0

    lax.fori_loop(0, rows // B, step, 0)


def chol_head_kernel(at_ref, *refs):
    pieces = refs[:8]
    lh, ll, ih, il, next_ref, uh, ul, s_ref, w_ref, v_ref = refs[8:]
    row = at_ref[0]
    col = at_ref[1]
    for par in range(2):
        @pl.when(row % 2 == par)
        def _():
            for k in range(16):
                here = pl.ds(pl.multiple_of(jnp.bitwise_xor(col, k) * PC, PC), PC)
                s_ref[here, 512 * par:512 * (par + 1)] = pieces[k // 4][k % 4]
                s_ref[here, 512 * (1 - par):512 * (2 - par)] = pieces[4 + k // 4][k % 4]
    for i in range(NB):
        for j in range(i, NB):
            up = s_ref[i * B:(i + 1) * B, j * B:(j + 1) * B]
            dn = s_ref[j * B:(j + 1) * B, i * B:(i + 1) * B]
            s_ref[i * B:(i + 1) * B, j * B:(j + 1) * B] = 0.5 * (up + dn.T)
    factor_blocks(HF, PB, s_ref, w_ref, v_ref, uh, ul, lh, ll, ih, il)
    left = (lh[HF:, :], ll[HF:, :])
    next_ref[...] = s_ref[HF:, HF:] - dot3(left, (uh[:, HF:], ul[:, HF:]))


def chol_tail_kernel(s_in, lh, ll, ih, il, uh, ul, s_ref, w_ref, v_ref):
    s_ref[...] = s_in[...]
    factor_blocks(HF, HF, s_ref, w_ref, v_ref, uh, ul, lh, ll, ih, il)


def chol_call(kernel, name, width, extra_out, args):
    part = jax.ShapeDtypeStruct((width, HF), bf16)
    inv = jax.ShapeDtypeStruct((HF // Q, Q, Q), bf16)
    vmem = pl.BlockSpec(memory_space=pltpu.VMEM)
    return pl.pallas_call(
        kernel,
        name=name,
        out_shape=(part, part, inv, inv) + extra_out,
        in_specs=[pl.BlockSpec(memory_space=pltpu.SMEM) if a.dtype == jnp.int32 else vmem for a in args],
        out_specs=(vmem,) * (4 + len(extra_out)),
        scratch_shapes=[
            pltpu.VMEM((HF, width), bf16),
            pltpu.VMEM((HF, width), bf16),
            pltpu.VMEM((width, width), f32),
            pltpu.VMEM((B, 2 * B), f32),
            pltpu.VMEM((2, B, B), f32),
        ],
        compiler_params=pltpu.CompilerParams(vmem_limit_bytes=58 * MB),
        cost_estimate=pl.CostEstimate(flops=25_000_000_000, transcendentals=0, bytes_accessed=8 * MB),
    )(*args)


def chol_head(at, pieces):
    nxt = jax.ShapeDtypeStruct((HF, HF), f32)
    return chol_call(chol_head_kernel, "chol_head", PB, (nxt,), [at, *pieces])


def chol_tail(nxt):
    return chol_call(chol_tail_kernel, "chol_tail", HF, (), [nxt])


def finish_kernel(at_ref, w0, w1, w2, w3, pan, trail,
                  lh1, ll1, ih1, il1, lh2, ll2, ih2, il2,
                  fac_out, out_out,
                  a_ref, p_ref, t_ref, lh, ll, ih, il, xh, xl, wh, wl,
                  fac_ref, out_ref, sem, pan_sem, trail_sem, out_sem):
    row = at_ref[0]
    col = at_ref[1]
    copy = pltpu.make_async_copy
    lo, hi = pl.ds(0, HF), pl.ds(HF, HF)
    factors = [
        copy(ih1, ih.at[pl.ds(0, 2)], sem.at[0]), copy(il1, il.at[pl.ds(0, 2)], sem.at[1]),
        copy(lh1, lh.at[:, lo], sem.at[2]), copy(ll1, ll.at[:, lo], sem.at[3]),
        copy(ih2, ih.at[pl.ds(2, 2)], sem.at[4]), copy(il2, il.at[pl.ds(2, 2)], sem.at[5]),
        copy(lh2, lh.at[hi, hi], sem.at[6]), copy(ll2, ll.at[hi, hi], sem.at[7]),
    ]
    window = []
    for k in range(8):
        here = pl.ds(pl.multiple_of(jnp.bitwise_xor(row, k) * B, B), B)
        window.append(copy((w0, w1, w2, w3)[k // 2].at[k % 2], a_ref.at[here], sem.at[8 + k]))
    def panel_copy(n):
        return copy(pan.at[:, pl.ds(n * 512, 512)], p_ref.at[n], pan_sem.at[n])

    def trail_copy(n):
        return copy(trail.at[pl.ds(n * 512, 512)], t_ref.at[n], trail_sem.at[n])

    def fac_copy(n):
        return copy(fac_ref.at[n], fac_out.at[:, pl.ds(n * 512, 512)], out_sem.at[n])

    def out_copy(n):
        return copy(out_ref.at[n], out_out.at[pl.ds(n * 512, 512)], out_sem.at[3 + n])

    for d in factors[:2] + window + factors[2:]:
        d.start()
    panel_copy(0).start()
    for n in range(3):
        if n:
            panel_copy(n).start()
        trail_copy(n).start()

    def solve(src, yh, yl, needs=((),) * 4):
        for k in range(PB // Q):
            for d in needs[k]:
                d.wait()
            here = slice(k * Q, (k + 1) * Q)
            v = src[here, :]
            if k:
                v = v - dot3((lh[here, :k * Q], ll[here, :k * Q]), (yh[:k * Q, :], yl[:k * Q, :]))
            yh[here, :], yl[here, :] = split(dot3((ih[k], il[k]), split(v)))

    solve(a_ref, wh, wl, (factors[:2] + window, factors[2:4], factors[4:6], factors[6:]))
    mine = pl.ds(pl.multiple_of(col * PC, PC), PC)

    def block(n, _):
        panel_copy(n).wait()
        own = jnp.logical_and(row == 0, n < 2)

        @pl.when(own)
        def _():
            here = pl.ds(pl.multiple_of(n * 512, 512), 512)
            xh[...] = lh[here, :].T
            xl[...] = ll[here, :].T

        @pl.when(jnp.logical_and(row == 0, n == 0))
        def _():
            xh[HF:, :] = jnp.zeros((HF, 512), bf16)
            xl[HF:, :] = jnp.zeros((HF, 512), bf16)

        @pl.when(jnp.logical_not(own))
        def _():
            solve(p_ref.at[n], xh, xl)

        fac_ref[n] = xh[mine, :].astype(f32) + xl[mine, :].astype(f32)
        fac_copy(n).start()
        prod = dot3((xh[...], xl[...]), (wh[...], wl[...]), LHS_T)
        trail_copy(n).wait()
        out_ref[n] = t_ref[n] - prod
        out_copy(n).start()
        return 0

    lax.fori_loop(0, 3, block, 0)
    for n in range(3):
        fac_copy(n).wait()
        out_copy(n).wait()


def finish(at, window, panel, trail, head, tail):
    hbm = pl.BlockSpec(memory_space=pl.ANY)
    dma = pltpu.SemaphoreType.DMA
    vm = pltpu.VMEM
    return pl.pallas_call(
        finish_kernel,
        name="finish",
        out_shape=(jax.ShapeDtypeStruct((PC, FR), f32), jax.ShapeDtypeStruct((FR, TC), f32)),
        in_specs=[pl.BlockSpec(memory_space=pltpu.SMEM)] + [hbm] * 14,
        out_specs=(hbm, hbm),
        scratch_shapes=[
            vm((PB, TC), f32), vm((3, PB, 512), f32), vm((3, 512, TC), f32),
            vm((PB, PB), bf16), vm((PB, PB), bf16),
            vm((PB // Q, Q, Q), bf16), vm((PB // Q, Q, Q), bf16),
            vm((PB, 512), bf16), vm((PB, 512), bf16), vm((PB, TC), bf16), vm((PB, TC), bf16),
            vm((3, PC, 512), f32), vm((3, 512, TC), f32),
            dma((16,)), dma((3,)), dma((3,)), dma((6,)),
        ],
        compiler_params=pltpu.CompilerParams(vmem_limit_bytes=58 * MB),
        cost_estimate=pl.CostEstimate(flops=15_000_000_000, transcendentals=0, bytes_accessed=25 * MB),
    )(at, *window, panel, trail, *head, *tail)


def flip(x, axis, bit, size):
    return lax.ppermute(x, axis, [(i, i ^ bit) for i in range(size)])


def window_pairs(step):
    pairs = []
    for c in range(16):
        for parity in range(2):
            if ((c + 2) % 3 + parity) % 3 == step:
                for r in range(8):
                    pairs.append((((c + 2) // 3) * 16 + 2 * r + parity, r * 16 + c))
    return pairs


def on_device(front_panel, front_trail, child_panel, child_trail, child_map, child_count):
    row = lax.axis_index("row")
    col = lax.axis_index("col")
    at = jnp.stack([row, col]).astype(jnp.int32)

    count = child_count.T
    own, send, crit = panel_parts(
        at, count, child_map, front_panel.T, child_panel.transpose(0, 2, 1)
    )
    there = lax.ppermute(crit, "row", [(0, 4), (4, 0)])
    there, send = lax.optimization_barrier((there, send))
    got = flip(send, "row", 4, 8)
    diag = crit + there
    lo, hi = diag[:, :512], diag[:, 512:]
    half = jnp.where(row % 4 == 0, lo, 0.0)
    for k, part in ((1, hi), (2, lo), (3, hi)):
        half = half + lax.ppermute(part, "row", [(0, k), (4, 4 + k)])
    x4 = jnp.stack([half] + [flip(half, "col", b, 16) for b in (1, 2, 3)])
    x4, got, count, child_a = lax.optimization_barrier((x4, got, count, child_trail[1, :EA]))
    child_a = flip(child_a, "row", 4, 8)
    mine = [x4] + [flip(x4, "col", b, 16) for b in (4, 8, 12)]
    panel_t = own + got[:PC]
    odd = jnp.bitwise_and(col, 1)
    panes = [panel_t[:, 512 * w:512 * (w + 1)] for w in range(3)]
    picks = [jnp.where(odd == 0, panes[k], panes[(k + 2) % 3]) for k in range(3)]
    trail = trail_own(count, child_map, front_trail, child_trail)
    *mine, panel_t, trail, child_a, child_b, p0, p1, p2 = lax.optimization_barrier(
        (*mine, panel_t, trail, child_a, child_trail[1, EA:], *picks)
    )
    panel_full = lax.all_gather(panel_t, "col", axis=0, tiled=True)
    other = [flip(piece, "row", 1, 8) for piece in mine]
    steps = [lax.ppermute(p, ("row", "col"), window_pairs(k)) for k, p in enumerate((p0, p1, p2))]
    child_b = flip(child_b, "row", 4, 8)

    *head, nxt = chol_head(at, mine + other)
    *steps, nxt, child_b = lax.optimization_barrier((*steps, nxt, child_b))
    at_w = (col + 2) % 3
    first = jnp.where(at_w == 0, steps[0], jnp.where(at_w == 1, steps[1], steps[2]))
    second = jnp.where(at_w == 0, steps[1], jnp.where(at_w == 1, steps[2], steps[0]))
    win = jnp.concatenate([first, second], axis=0)
    pair = jnp.stack([win, flip(win, "row", 1, 8)])
    window = [pair] + [flip(pair, "row", b, 8) for b in (2, 4, 6)]
    tail = chol_tail(nxt)

    trail = trail_got(got, trail, child_a, child_b)
    factor_t, schur = finish(at, window, panel_full, trail, head, tail)
    return factor_t.T, schur


def solution(mesh):
    in_specs = (
        P("row", "col"),
        P("row", "col"),
        P(None, "row", "col"),
        P(None, "row", "col"),
        P(None, "row"),
        P(None, "row"),
    )
    out_specs = (P("row", "col"), P("row", "col"))
    return jax.shard_map(
        on_device, mesh=mesh, in_specs=in_specs, out_specs=out_specs, check_vma=False
    )
```

```python
import jax
import jax.numpy as jnp
from jax import lax
from jax.experimental import pallas as pl
from jax.experimental.pallas import tpu as pltpu
from jax.sharding import PartitionSpec as P

f32 = jnp.float32
bf16 = jnp.bfloat16

F = 12288
PB = 1024
CR = 1024
FR = 1536
TC = 512
PC = 64
B = 128
NB = PB // B
Q = 256
HF = 512
EA = 544
MB = 1 << 20

NATURAL = (((1,), (0,)), ((), ()))
LHS_T = (((0,), (0,)), ((), ()))
RHS_T = (((1,), (1,)), ((), ()))


def split(x):
    hi = x.astype(bf16)
    return hi, (x - hi.astype(f32)).astype(bf16)


def dot1(a, b, dims=NATURAL):
    return lax.dot_general(a, b, dims, preferred_element_type=f32)


def dot3(a, b, dims=NATURAL):
    (ah, al), (bh, bl) = a, b
    return dot1(ah, bh, dims) + (dot1(ah, bl, dims) + dot1(al, bh, dims))


def one_hot(first, rows, target):
    at = first + lax.broadcasted_iota(jnp.int32, (rows, CR), 0)
    return (at == target).astype(f32).astype(bf16)


def live_target(count, map_row):
    k = lax.broadcasted_iota(jnp.int32, (1, CR), 1)
    return jnp.where(k < count, map_row, -1)


def panel_kernel(at_ref, count_ref, map_ref, front_ref, child_ref, own_ref, send_ref, crit_ref):
    for slab in range(2):
        target = live_target(count_ref[0, slab], map_ref[slab:slab + 1, :])
        c = child_ref[slab]
        hi = c.astype(bf16)
        rest = c - hi.astype(f32)
        mid = rest.astype(bf16)
        low = (rest - mid.astype(f32)).astype(bf16)
        parts = jnp.concatenate([hi, mid, low], axis=0)
        for at in range(0, FR, 512):
            moved = dot1(parts, one_hot(at, 512, target), RHS_T)
            moved = moved[:PC] + (moved[PC:2 * PC] + moved[2 * PC:])
            if slab == 0:
                own_ref[:, at:at + 512] = front_ref[:, at:at + 512] + moved
            else:
                send_ref[:PC, at:at + 512] = moved
        if slab == 1:
            send_ref[PC:, :CR] = jnp.broadcast_to(target.astype(f32), (8, CR))
            send_ref[PC:, CR:] = jnp.zeros((8, FR - CR), f32)
    crit_ref[...] = send_ref[:PC, :PB]

    @pl.when(at_ref[0] == 0)
    def _():
        crit_ref[...] = own_ref[:, :PB]


def panel_parts(at, count, child_map, front_t, child_t):
    return pl.pallas_call(
        panel_kernel,
        name="panel_parts",
        out_shape=(
            jax.ShapeDtypeStruct((PC, FR), f32),
            jax.ShapeDtypeStruct((PC + 8, FR), f32),
            jax.ShapeDtypeStruct((PC, PB), f32),
        ),
        in_specs=[pl.BlockSpec(memory_space=pltpu.SMEM)] * 2 + [pl.BlockSpec(memory_space=pltpu.VMEM)] * 3,
        out_specs=(pl.BlockSpec(memory_space=pltpu.VMEM),) * 3,
        compiler_params=pltpu.CompilerParams(vmem_limit_bytes=58 * MB),
    )(at, count, child_map, front_t, child_t)


def trail_kernel(count_ref, map_ref, front_ref, child_ref, out_ref, ch, cl):
    @pl.when(pl.program_id(0) == 0)
    def _():
        ch[...], cl[...] = split(child_ref[...])

    target = live_target(count_ref[0, 0], map_ref[0:1, :])
    g = one_hot(pl.program_id(0) * 512, 512, target)
    out_ref[...] = front_ref[...] + (dot1(g, ch[...]) + dot1(g, cl[...]))


def trail_own(count, child_map, front, child):
    return pl.pallas_call(
        trail_kernel,
        name="trail_own",
        grid=(FR // 512,),
        out_shape=jax.ShapeDtypeStruct((FR, TC), f32),
        in_specs=[
            pl.BlockSpec(memory_space=pltpu.SMEM),
            pl.BlockSpec((2, CR), lambda s: (0, 0)),
            pl.BlockSpec((512, TC), lambda s: (s, 0)),
            pl.BlockSpec((None, CR, TC), lambda s: (0, 0, 0)),
        ],
        out_specs=pl.BlockSpec((512, TC), lambda s: (s, 0)),
        scratch_shapes=[pltpu.VMEM((CR, TC), bf16)] * 2,
        compiler_params=pltpu.CompilerParams(vmem_limit_bytes=58 * MB),
    )(count, child_map, front, child)


def trail_got_kernel(got_ref, trail_ref, a_ref, b_ref, out_ref, ch, cl):
    @pl.when(pl.program_id(0) == 0)
    def _():
        ch[:EA, :], cl[:EA, :] = split(a_ref[...])
        ch[EA:, :], cl[EA:, :] = split(b_ref[...])

    target = got_ref[0:1, :CR].astype(jnp.int32)
    g = one_hot(pl.program_id(0) * 256, 256, target)
    out_ref[...] = trail_ref[...] + (dot1(g, ch[...]) + dot1(g, cl[...]))


def trail_got(got, trail, child_a, child_b):
    return pl.pallas_call(
        trail_got_kernel,
        name="trail_got",
        grid=(FR // 256,),
        out_shape=jax.ShapeDtypeStruct((FR, TC), f32),
        in_specs=[
            pl.BlockSpec((8, FR), lambda s: (PC // 8, 0)),
            pl.BlockSpec((256, TC), lambda s: (s, 0)),
            pl.BlockSpec((EA, TC), lambda s: (0, 0)),
            pl.BlockSpec((CR - EA, TC), lambda s: (0, 0)),
        ],
        out_specs=pl.BlockSpec((256, TC), lambda s: (s, 0)),
        scratch_shapes=[pltpu.VMEM((CR, TC), bf16)] * 2,
        compiler_params=pltpu.CompilerParams(vmem_limit_bytes=58 * MB),
    )(got, trail, child_a, child_b)


def lane(x, at):
    return jnp.broadcast_to(x[:, at:at + 1], (8, B))


def chain(w_ref):
    sub = lax.broadcasted_iota(jnp.int32, (8, B), 0)
    for m in range(B // 8):
        here = slice(8 * m, 8 * m + 8)
        p, a = [], []
        for i in range(8):
            x = jnp.broadcast_to(w_ref[8 * m + i:8 * m + i + 1, :], (8, 2 * B))
            p.append(x[:, :B])
            a.append(x[:, B:])
        d = {(i, j): lane(p[i], 8 * m + j) for i in range(8) for j in range(i + 1)}
        near = m + 1 < B // 8
        if near:
            at = slice(8 * m + 8, 8 * m + 16)
            np_, na = w_ref[at, :B], w_ref[at, B:]
            c = [lane(np_, 8 * m + j) for j in range(8)]
        u, v, r, low = [], [], [], {}
        for j in range(8):
            r.append(lax.rsqrt(d[j, j]))
            for i in range(j + 1, 8):
                low[i, j] = d[i, j] * r[j]
            for i in range(j + 1, 8):
                for k in range(j + 1, i + 1):
                    d[i, k] = d[i, k] - low[i, j] * low[k, j]
            u.append(p[j] * r[j])
            v.append(a[j] * r[j])
            for i in range(j + 1, 8):
                p[i] = p[i] - low[i, j] * u[j]
                a[i] = a[i] - low[i, j] * v[j]
            if near:
                cj = c[j] * r[j]
                for i in range(j + 1, 8):
                    c[i] = c[i] - low[i, j] * cj
                np_ = np_ - cj * u[j]
                na = na - cj * v[j]
        if near:
            w_ref[at, :B] = np_
            w_ref[at, B:] = na
        cu, cv = u[0], v[0]
        for j in range(1, 8):
            cu = jnp.where(sub == j, u[j], cu)
            cv = jnp.where(sub == j, v[j], cv)
        w_ref[here, :B] = cu
        w_ref[here, B:] = cv
        if m + 2 < B // 8:
            for n in range(m + 2, B // 8):
                at = slice(8 * n, 8 * n + 8)
                x, y = w_ref[at, :B], w_ref[at, B:]
                c = [lane(x, 8 * m + j) for j in range(8)]
                g, h = u, v
                for j in range(8):
                    c[j] = c[j] * r[j]
                    for i in range(j + 1, 8):
                        c[i] = c[i] - low[i, j] * c[j]
                sx = [c[j] * g[j] for j in range(8)]
                sy = [c[j] * h[j] for j in range(8)]
                while len(sx) > 1:
                    sx = [sx[k] + sx[k + 1] for k in range(0, len(sx), 2)]
                    sy = [sy[k] + sy[k + 1] for k in range(0, len(sy), 2)]
                w_ref[at, :B] = x - sx[0]
                w_ref[at, B:] = y - sy[0]


def factor_blocks(rows, width, s_ref, w_ref, v_ref, uh, ul, lh, ll, ih, il):
    r = lax.broadcasted_iota(jnp.int32, (B, B), 0)
    c = lax.broadcasted_iota(jnp.int32, (B, B), 1)
    eye = (r == c).astype(f32)

    def step(k, _):
        for kk in range(rows // B):
            @pl.when(k == kk)
            def _():
                here = slice(kk * B, (kk + 1) * B)
                if kk:
                    left = (lh[here, :kk * B], ll[here, :kk * B])
                    right = (uh[:kk * B, kk * B:], ul[:kk * B, kk * B:])
                    s_ref[here, kk * B:] = s_ref[here, kk * B:] - dot3(left, right)
                w_ref[:, :B] = s_ref[here, here]

        w_ref[:, B:] = eye
        chain(w_ref)
        v = w_ref[:, B:]
        v_ref[k % 2] = v
        vs = split(v)
        for kk in range(rows // B):
            @pl.when(k == kk)
            def _():
                here = slice(kk * B, (kk + 1) * B)
                rest = slice((kk + 1) * B, width)
                dh, dl = split(jnp.where(r <= c, w_ref[:, :B], 0.0))
                lh[here, here] = dh.T
                ll[here, here] = dl.T
                if kk < width // B - 1:
                    rh, rl = split(dot3(vs, split(s_ref[here, rest])))
                    uh[here, rest] = rh
                    ul[here, rest] = rl
                    lh[rest, here] = rh.T
                    ll[rest, here] = rl.T
                if kk < rows // B - 1:
                    lh[here, (kk + 1) * B:rows] = jnp.zeros((B, rows - (kk + 1) * B), bf16)
                    ll[here, (kk + 1) * B:rows] = jnp.zeros((B, rows - (kk + 1) * B), bf16)
                half = kk % 2
                at = half * B
                ih[kk // 2, at:at + B, at:at + B] = vs[0]
                il[kk // 2, at:at + B, at:at + B] = vs[1]
                if half:
                    before = slice((kk - 1) * B, kk * B)
                    first = split(v_ref[0])
                    cross = split(dot3((lh[here, before], ll[here, before]), first))
                    th, tl = split(-dot3(vs, cross))
                    ih[kk // 2, B:, :B] = th
                    il[kk // 2, B:, :B] = tl
                    ih[kk // 2, :B, B:] = jnp.zeros((B, B), bf16)
                    il[kk // 2, :B, B:] = jnp.zeros((B, B), bf16)
        return 0

    lax.fori_loop(0, rows // B, step, 0)


def chol_head_kernel(at_ref, *refs):
    pieces = refs[:8]
    lh, ll, ih, il, next_ref, uh, ul, s_ref, w_ref, v_ref = refs[8:]
    row = at_ref[0]
    col = at_ref[1]
    for par in range(2):
        @pl.when(row % 2 == par)
        def _():
            for k in range(16):
                here = pl.ds(pl.multiple_of(jnp.bitwise_xor(col, k) * PC, PC), PC)
                s_ref[here, 512 * par:512 * (par + 1)] = pieces[k // 4][k % 4]
                s_ref[here, 512 * (1 - par):512 * (2 - par)] = pieces[4 + k // 4][k % 4]
    for i in range(NB):
        for j in range(i, NB):
            up = s_ref[i * B:(i + 1) * B, j * B:(j + 1) * B]
            dn = s_ref[j * B:(j + 1) * B, i * B:(i + 1) * B]
            s_ref[i * B:(i + 1) * B, j * B:(j + 1) * B] = 0.5 * (up + dn.T)
    factor_blocks(HF, PB, s_ref, w_ref, v_ref, uh, ul, lh, ll, ih, il)
    left = (lh[HF:, :], ll[HF:, :])
    next_ref[...] = s_ref[HF:, HF:] - dot3(left, (uh[:, HF:], ul[:, HF:]))


def chol_tail_kernel(s_in, lh, ll, ih, il, uh, ul, s_ref, w_ref, v_ref):
    s_ref[...] = s_in[...]
    factor_blocks(HF, HF, s_ref, w_ref, v_ref, uh, ul, lh, ll, ih, il)


def chol_call(kernel, name, width, extra_out, args):
    part = jax.ShapeDtypeStruct((width, HF), bf16)
    inv = jax.ShapeDtypeStruct((HF // Q, Q, Q), bf16)
    vmem = pl.BlockSpec(memory_space=pltpu.VMEM)
    return pl.pallas_call(
        kernel,
        name=name,
        out_shape=(part, part, inv, inv) + extra_out,
        in_specs=[pl.BlockSpec(memory_space=pltpu.SMEM) if a.dtype == jnp.int32 else vmem for a in args],
        out_specs=(vmem,) * (4 + len(extra_out)),
        scratch_shapes=[
            pltpu.VMEM((HF, width), bf16),
            pltpu.VMEM((HF, width), bf16),
            pltpu.VMEM((width, width), f32),
            pltpu.VMEM((B, 2 * B), f32),
            pltpu.VMEM((2, B, B), f32),
        ],
        compiler_params=pltpu.CompilerParams(vmem_limit_bytes=58 * MB),
        cost_estimate=pl.CostEstimate(flops=25_000_000_000, transcendentals=0, bytes_accessed=8 * MB),
    )(*args)


def chol_head(at, pieces):
    nxt = jax.ShapeDtypeStruct((HF, HF), f32)
    return chol_call(chol_head_kernel, "chol_head", PB, (nxt,), [at, *pieces])


def chol_tail(nxt):
    return chol_call(chol_tail_kernel, "chol_tail", HF, (), [nxt])


def finish_kernel(at_ref, w0, w1, w2, w3, pan, trail,
                  lh1, ll1, ih1, il1, lh2, ll2, ih2, il2,
                  fac_out, out_out,
                  a_ref, p_ref, t_ref, lh, ll, ih, il, xh, xl, wh, wl,
                  fac_ref, out_ref, sem, pan_sem, trail_sem, out_sem):
    row = at_ref[0]
    col = at_ref[1]
    copy = pltpu.make_async_copy
    lo, hi = pl.ds(0, HF), pl.ds(HF, HF)
    factors = [
        copy(ih1, ih.at[pl.ds(0, 2)], sem.at[0]), copy(il1, il.at[pl.ds(0, 2)], sem.at[1]),
        copy(lh1, lh.at[:, lo], sem.at[2]), copy(ll1, ll.at[:, lo], sem.at[3]),
        copy(ih2, ih.at[pl.ds(2, 2)], sem.at[4]), copy(il2, il.at[pl.ds(2, 2)], sem.at[5]),
        copy(lh2, lh.at[hi, hi], sem.at[6]), copy(ll2, ll.at[hi, hi], sem.at[7]),
    ]
    window = []
    for k in range(8):
        here = pl.ds(pl.multiple_of(jnp.bitwise_xor(row, k) * B, B), B)
        window.append(copy((w0, w1, w2, w3)[k // 2].at[k % 2], a_ref.at[here], sem.at[8 + k]))
    def panel_copy(n):
        return copy(pan.at[:, pl.ds(n * 512, 512)], p_ref.at[n], pan_sem.at[n])

    def trail_copy(n):
        return copy(trail.at[pl.ds(n * 512, 512)], t_ref.at[n], trail_sem.at[n])

    def fac_copy(n):
        return copy(fac_ref.at[n], fac_out.at[:, pl.ds(n * 512, 512)], out_sem.at[n])

    def out_copy(n):
        return copy(out_ref.at[n], out_out.at[pl.ds(n * 512, 512)], out_sem.at[3 + n])

    for d in factors[:2] + window + factors[2:]:
        d.start()
    panel_copy(0).start()
    for n in range(3):
        if n:
            panel_copy(n).start()
        trail_copy(n).start()

    def solve(src, yh, yl, needs=((),) * 4):
        for k in range(PB // Q):
            for d in needs[k]:
                d.wait()
            here = slice(k * Q, (k + 1) * Q)
            v = src[here, :]
            if k:
                v = v - dot3((lh[here, :k * Q], ll[here, :k * Q]), (yh[:k * Q, :], yl[:k * Q, :]))
            yh[here, :], yl[here, :] = split(dot3((ih[k], il[k]), split(v)))

    solve(a_ref, wh, wl, (factors[:2] + window, factors[2:4], factors[4:6], factors[6:]))
    mine = pl.ds(pl.multiple_of(col * PC, PC), PC)

    def block(n, _):
        panel_copy(n).wait()
        own = jnp.logical_and(row == 0, n < 2)

        @pl.when(own)
        def _():
            here = pl.ds(pl.multiple_of(n * 512, 512), 512)
            xh[...] = lh[here, :].T
            xl[...] = ll[here, :].T

        @pl.when(jnp.logical_and(row == 0, n == 0))
        def _():
            xh[HF:, :] = jnp.zeros((HF, 512), bf16)
            xl[HF:, :] = jnp.zeros((HF, 512), bf16)

        @pl.when(jnp.logical_not(own))
        def _():
            solve(p_ref.at[n], xh, xl)

        fac_ref[n] = xh[mine, :].astype(f32) + xl[mine, :].astype(f32)
        fac_copy(n).start()
        prod = dot3((xh[...], xl[...]), (wh[...], wl[...]), LHS_T)
        trail_copy(n).wait()
        out_ref[n] = t_ref[n] - prod
        out_copy(n).start()
        return 0

    lax.fori_loop(0, 3, block, 0)
    for n in range(3):
        fac_copy(n).wait()
        out_copy(n).wait()


def finish(at, window, panel, trail, head, tail):
    hbm = pl.BlockSpec(memory_space=pl.ANY)
    dma = pltpu.SemaphoreType.DMA
    vm = pltpu.VMEM
    return pl.pallas_call(
        finish_kernel,
        name="finish",
        out_shape=(jax.ShapeDtypeStruct((PC, FR), f32), jax.ShapeDtypeStruct((FR, TC), f32)),
        in_specs=[pl.BlockSpec(memory_space=pltpu.SMEM)] + [hbm] * 14,
        out_specs=(hbm, hbm),
        scratch_shapes=[
            vm((PB, TC), f32), vm((3, PB, 512), f32), vm((3, 512, TC), f32),
            vm((PB, PB), bf16), vm((PB, PB), bf16),
            vm((PB // Q, Q, Q), bf16), vm((PB // Q, Q, Q), bf16),
            vm((PB, 512), bf16), vm((PB, 512), bf16), vm((PB, TC), bf16), vm((PB, TC), bf16),
            vm((3, PC, 512), f32), vm((3, 512, TC), f32),
            dma((16,)), dma((3,)), dma((3,)), dma((6,)),
        ],
        compiler_params=pltpu.CompilerParams(vmem_limit_bytes=58 * MB),
        cost_estimate=pl.CostEstimate(flops=15_000_000_000, transcendentals=0, bytes_accessed=25 * MB),
    )(at, *window, panel, trail, *head, *tail)


def flip(x, axis, bit, size):
    return lax.ppermute(x, axis, [(i, i ^ bit) for i in range(size)])


def window_pairs(step):
    pairs = []
    for c in range(16):
        for parity in range(2):
            if ((c + 2) % 3 + parity) % 3 == step:
                for r in range(8):
                    pairs.append((((c + 2) // 3) * 16 + 2 * r + parity, r * 16 + c))
    return pairs


def on_device(front_panel, front_trail, child_panel, child_trail, child_map, child_count):
    row = lax.axis_index("row")
    col = lax.axis_index("col")
    at = jnp.stack([row, col]).astype(jnp.int32)

    count = child_count.T
    own, send, crit = panel_parts(
        at, count, child_map, front_panel.T, child_panel.transpose(0, 2, 1)
    )
    there = lax.ppermute(crit, "row", [(0, 4), (4, 0)])
    there, send = lax.optimization_barrier((there, send))
    got = flip(send, "row", 4, 8)
    diag = crit + there
    lo, hi = diag[:, :512], diag[:, 512:]
    half = jnp.where(row % 4 == 0, lo, 0.0)
    for k, part in ((1, hi), (2, lo), (3, hi)):
        half = half + lax.ppermute(part, "row", [(0, k), (4, 4 + k)])
    x4 = jnp.stack([half] + [flip(half, "col", b, 16) for b in (1, 2, 3)])
    x4, got, count, child_a = lax.optimization_barrier((x4, got, count, child_trail[1, :EA]))
    child_a = flip(child_a, "row", 4, 8)
    mine = [x4] + [flip(x4, "col", b, 16) for b in (4, 8, 12)]
    panel_t = own + got[:PC]
    odd = jnp.bitwise_and(col, 1)
    panes = [panel_t[:, 512 * w:512 * (w + 1)] for w in range(3)]
    picks = [jnp.where(odd == 0, panes[k], panes[(k + 2) % 3]) for k in range(3)]
    trail = trail_own(count, child_map, front_trail, child_trail)
    *mine, panel_t, trail, child_a, child_b, p0, p1, p2 = lax.optimization_barrier(
        (*mine, panel_t, trail, child_a, child_trail[1, EA:], *picks)
    )
    panel_full = lax.all_gather(panel_t, "col", axis=0, tiled=True)
    other = [flip(piece, "row", 1, 8) for piece in mine]
    steps = [lax.ppermute(p, ("row", "col"), window_pairs(k)) for k, p in enumerate((p0, p1, p2))]
    child_b = flip(child_b, "row", 4, 8)

    *head, nxt = chol_head(at, mine + other)
    *steps, nxt, child_b = lax.optimization_barrier((*steps, nxt, child_b))
    at_w = (col + 2) % 3
    first = jnp.where(at_w == 0, steps[0], jnp.where(at_w == 1, steps[1], steps[2]))
    second = jnp.where(at_w == 0, steps[1], jnp.where(at_w == 1, steps[2], steps[0]))
    win = jnp.concatenate([first, second], axis=0)
    pair = jnp.stack([win, flip(win, "row", 1, 8)])
    window = [pair] + [flip(pair, "row", b, 8) for b in (2, 4, 6)]
    tail = chol_tail(nxt)

    trail = trail_got(got, trail, child_a, child_b)
    factor_t, schur = finish(at, window, panel_full, trail, head, tail)
    return factor_t.T, schur


def solution(mesh):
    in_specs = (
        P("row", "col"),
        P("row", "col"),
        P(None, "row", "col"),
        P(None, "row", "col"),
        P(None, "row"),
        P(None, "row"),
    )
    out_specs = (P("row", "col"), P("row", "col"))
    return jax.shard_map(
        on_device, mesh=mesh, in_specs=in_specs, out_specs=out_specs, check_vma=False
    )
```

```python
import jax
import jax.numpy as jnp
from jax import lax
from jax.experimental import pallas as pl
from jax.experimental.pallas import tpu as pltpu
from jax.sharding import PartitionSpec as P

f32 = jnp.float32
bf16 = jnp.bfloat16

F = 12288
PB = 1024
CR = 1024
FR = 1536
TC = 512
PC = 64
B = 128
NB = PB // B
Q = 256
HF = 512
EA = 544
MB = 1 << 20

NATURAL = (((1,), (0,)), ((), ()))
LHS_T = (((0,), (0,)), ((), ()))
RHS_T = (((1,), (1,)), ((), ()))


def split(x):
    hi = x.astype(bf16)
    return hi, (x - hi.astype(f32)).astype(bf16)


def dot1(a, b, dims=NATURAL):
    return lax.dot_general(a, b, dims, preferred_element_type=f32)


def dot3(a, b, dims=NATURAL):
    (ah, al), (bh, bl) = a, b
    return dot1(ah, bh, dims) + (dot1(ah, bl, dims) + dot1(al, bh, dims))


def one_hot(first, rows, target):
    at = first + lax.broadcasted_iota(jnp.int32, (rows, CR), 0)
    return (at == target).astype(f32).astype(bf16)


def live_target(count, map_row):
    k = lax.broadcasted_iota(jnp.int32, (1, CR), 1)
    return jnp.where(k < count, map_row, -1)


def panel_kernel(at_ref, count_ref, map_ref, front_ref, child_ref, own_ref, send_ref, crit_ref):
    for slab in range(2):
        target = live_target(count_ref[0, slab], map_ref[slab:slab + 1, :])
        c = child_ref[slab]
        parts = jnp.concatenate(split(c), axis=0)
        for at in range(0, FR, 512):
            moved = dot1(parts, one_hot(at, 512, target), RHS_T)
            moved = moved[:PC] + moved[PC:]
            if slab == 0:
                own_ref[:, at:at + 512] = front_ref[:, at:at + 512] + moved
            else:
                send_ref[:PC, at:at + 512] = moved
        if slab == 1:
            send_ref[PC:, :CR] = jnp.broadcast_to(target.astype(f32), (8, CR))
            send_ref[PC:, CR:] = jnp.zeros((8, FR - CR), f32)
    crit_ref[...] = send_ref[:PC, :PB]

    @pl.when(at_ref[0] == 0)
    def _():
        crit_ref[...] = own_ref[:, :PB]


def panel_parts(at, count, child_map, front_t, child_t):
    return pl.pallas_call(
        panel_kernel,
        name="panel_parts",
        out_shape=(
            jax.ShapeDtypeStruct((PC, FR), f32),
            jax.ShapeDtypeStruct((PC + 8, FR), f32),
            jax.ShapeDtypeStruct((PC, PB), f32),
        ),
        in_specs=[pl.BlockSpec(memory_space=pltpu.SMEM)] * 2 + [pl.BlockSpec(memory_space=pltpu.VMEM)] * 3,
        out_specs=(pl.BlockSpec(memory_space=pltpu.VMEM),) * 3,
        compiler_params=pltpu.CompilerParams(vmem_limit_bytes=58 * MB),
    )(at, count, child_map, front_t, child_t)


def trail_kernel(count_ref, map_ref, front_ref, child_ref, out_ref, ch, cl):
    @pl.when(pl.program_id(0) == 0)
    def _():
        ch[...], cl[...] = split(child_ref[...])

    target = live_target(count_ref[0, 0], map_ref[0:1, :])
    g = one_hot(pl.program_id(0) * 512, 512, target)
    out_ref[...] = front_ref[...] + (dot1(g, ch[...]) + dot1(g, cl[...]))


def trail_own(count, child_map, front, child):
    return pl.pallas_call(
        trail_kernel,
        name="trail_own",
        grid=(FR // 512,),
        out_shape=jax.ShapeDtypeStruct((FR, TC), f32),
        in_specs=[
            pl.BlockSpec(memory_space=pltpu.SMEM),
            pl.BlockSpec((2, CR), lambda s: (0, 0)),
            pl.BlockSpec((512, TC), lambda s: (s, 0)),
            pl.BlockSpec((None, CR, TC), lambda s: (0, 0, 0)),
        ],
        out_specs=pl.BlockSpec((512, TC), lambda s: (s, 0)),
        scratch_shapes=[pltpu.VMEM((CR, TC), bf16)] * 2,
        compiler_params=pltpu.CompilerParams(vmem_limit_bytes=58 * MB),
    )(count, child_map, front, child)


def trail_got_kernel(got_ref, trail_ref, a_ref, b_ref, out_ref, ch, cl):
    @pl.when(pl.program_id(0) == 0)
    def _():
        ch[:EA, :], cl[:EA, :] = split(a_ref[...])
        ch[EA:, :], cl[EA:, :] = split(b_ref[...])

    target = got_ref[0:1, :CR].astype(jnp.int32)
    g = one_hot(pl.program_id(0) * 512, 512, target)
    out_ref[...] = trail_ref[...] + (dot1(g, ch[...]) + dot1(g, cl[...]))


def trail_got(got, trail, child_a, child_b):
    return pl.pallas_call(
        trail_got_kernel,
        name="trail_got",
        grid=(FR // 512,),
        out_shape=jax.ShapeDtypeStruct((FR, TC), f32),
        in_specs=[
            pl.BlockSpec((8, FR), lambda s: (PC // 8, 0)),
            pl.BlockSpec((512, TC), lambda s: (s, 0)),
            pl.BlockSpec((EA, TC), lambda s: (0, 0)),
            pl.BlockSpec((CR - EA, TC), lambda s: (0, 0)),
        ],
        out_specs=pl.BlockSpec((512, TC), lambda s: (s, 0)),
        scratch_shapes=[pltpu.VMEM((CR, TC), bf16)] * 2,
        compiler_params=pltpu.CompilerParams(vmem_limit_bytes=58 * MB),
    )(got, trail, child_a, child_b)


def lane(x, at):
    return jnp.broadcast_to(x[:, at:at + 1], (8, B))


def chain(w_ref):
    sub = lax.broadcasted_iota(jnp.int32, (8, B), 0)
    for m in range(B // 8):
        here = slice(8 * m, 8 * m + 8)
        p, a = [], []
        for i in range(8):
            x = jnp.broadcast_to(w_ref[8 * m + i:8 * m + i + 1, :], (8, 2 * B))
            p.append(x[:, :B])
            a.append(x[:, B:])
        d = {(i, j): lane(p[i], 8 * m + j) for i in range(8) for j in range(i + 1)}
        near = m + 1 < B // 8
        if near:
            at = slice(8 * m + 8, 8 * m + 16)
            np_, na = w_ref[at, :B], w_ref[at, B:]
            c = [lane(np_, 8 * m + j) for j in range(8)]
        u, v, r, low = [], [], [], {}
        for j in range(8):
            r.append(lax.rsqrt(d[j, j]))
            for i in range(j + 1, 8):
                low[i, j] = d[i, j] * r[j]
            for i in range(j + 1, 8):
                for k in range(j + 1, i + 1):
                    d[i, k] = d[i, k] - low[i, j] * low[k, j]
            u.append(p[j] * r[j])
            v.append(a[j] * r[j])
            for i in range(j + 1, 8):
                p[i] = p[i] - low[i, j] * u[j]
                a[i] = a[i] - low[i, j] * v[j]
            if near:
                cj = c[j] * r[j]
                for i in range(j + 1, 8):
                    c[i] = c[i] - low[i, j] * cj
                np_ = np_ - cj * u[j]
                na = na - cj * v[j]
        if near:
            w_ref[at, :B] = np_
            w_ref[at, B:] = na
        cu, cv = u[0], v[0]
        for j in range(1, 8):
            cu = jnp.where(sub == j, u[j], cu)
            cv = jnp.where(sub == j, v[j], cv)
        w_ref[here, :B] = cu
        w_ref[here, B:] = cv
        if m + 2 < B // 8:
            for n in range(m + 2, B // 8):
                at = slice(8 * n, 8 * n + 8)
                x, y = w_ref[at, :B], w_ref[at, B:]
                c = [lane(x, 8 * m + j) for j in range(8)]
                g, h = u, v
                for j in range(8):
                    c[j] = c[j] * r[j]
                    for i in range(j + 1, 8):
                        c[i] = c[i] - low[i, j] * c[j]
                sx = [c[j] * g[j] for j in range(8)]
                sy = [c[j] * h[j] for j in range(8)]
                while len(sx) > 1:
                    sx = [sx[k] + sx[k + 1] for k in range(0, len(sx), 2)]
                    sy = [sy[k] + sy[k + 1] for k in range(0, len(sy), 2)]
                w_ref[at, :B] = x - sx[0]
                w_ref[at, B:] = y - sy[0]


def factor_blocks(rows, width, s_ref, w_ref, v_ref, uh, ul, lh, ll, ih, il):
    r = lax.broadcasted_iota(jnp.int32, (B, B), 0)
    c = lax.broadcasted_iota(jnp.int32, (B, B), 1)
    eye = (r == c).astype(f32)

    def step(k, _):
        for kk in range(rows // B):
            @pl.when(k == kk)
            def _():
                here = slice(kk * B, (kk + 1) * B)
                if kk:
                    left = (lh[here, :kk * B], ll[here, :kk * B])
                    right = (uh[:kk * B, kk * B:], ul[:kk * B, kk * B:])
                    s_ref[here, kk * B:] = s_ref[here, kk * B:] - dot3(left, right)
                w_ref[:, :B] = s_ref[here, here]

        w_ref[:, B:] = eye
        chain(w_ref)
        v = w_ref[:, B:]
        v_ref[k % 2] = v
        vs = split(v)
        for kk in range(rows // B):
            @pl.when(k == kk)
            def _():
                here = slice(kk * B, (kk + 1) * B)
                rest = slice((kk + 1) * B, width)
                dh, dl = split(jnp.where(r <= c, w_ref[:, :B], 0.0))
                lh[here, here] = dh.T
                ll[here, here] = dl.T
                if kk < width // B - 1:
                    rh, rl = split(dot3(vs, split(s_ref[here, rest])))
                    uh[here, rest] = rh
                    ul[here, rest] = rl
                    lh[rest, here] = rh.T
                    ll[rest, here] = rl.T
                if kk < rows // B - 1:
                    lh[here, (kk + 1) * B:rows] = jnp.zeros((B, rows - (kk + 1) * B), bf16)
                    ll[here, (kk + 1) * B:rows] = jnp.zeros((B, rows - (kk + 1) * B), bf16)
                half = kk % 2
                at = half * B
                ih[kk // 2, at:at + B, at:at + B] = vs[0]
                il[kk // 2, at:at + B, at:at + B] = vs[1]
                if half:
                    before = slice((kk - 1) * B, kk * B)
                    first = split(v_ref[0])
                    cross = split(dot3((lh[here, before], ll[here, before]), first))
                    th, tl = split(-dot3(vs, cross))
                    ih[kk // 2, B:, :B] = th
                    il[kk // 2, B:, :B] = tl
                    ih[kk // 2, :B, B:] = jnp.zeros((B, B), bf16)
                    il[kk // 2, :B, B:] = jnp.zeros((B, B), bf16)
        return 0

    lax.fori_loop(0, rows // B, step, 0)


def chol_head_kernel(at_ref, *refs):
    pieces = refs[:8]
    lh, ll, ih, il, next_ref, uh, ul, s_ref, w_ref, v_ref = refs[8:]
    row = at_ref[0]
    col = at_ref[1]
    for par in range(2):
        @pl.when(row % 2 == par)
        def _():
            for k in range(16):
                here = pl.ds(pl.multiple_of(jnp.bitwise_xor(col, k) * PC, PC), PC)
                s_ref[here, 512 * par:512 * (par + 1)] = pieces[k // 4][k % 4]
                s_ref[here, 512 * (1 - par):512 * (2 - par)] = pieces[4 + k // 4][k % 4]
    for i in range(NB):
        for j in range(i, NB):
            up = s_ref[i * B:(i + 1) * B, j * B:(j + 1) * B]
            dn = s_ref[j * B:(j + 1) * B, i * B:(i + 1) * B]
            s_ref[i * B:(i + 1) * B, j * B:(j + 1) * B] = 0.5 * (up + dn.T)
    factor_blocks(HF, PB, s_ref, w_ref, v_ref, uh, ul, lh, ll, ih, il)
    left = (lh[HF:, :], ll[HF:, :])
    next_ref[...] = s_ref[HF:, HF:] - dot3(left, (uh[:, HF:], ul[:, HF:]))


def chol_tail_kernel(s_in, lh, ll, ih, il, uh, ul, s_ref, w_ref, v_ref):
    s_ref[...] = s_in[...]
    factor_blocks(HF, HF, s_ref, w_ref, v_ref, uh, ul, lh, ll, ih, il)


def chol_call(kernel, name, width, extra_out, args):
    part = jax.ShapeDtypeStruct((width, HF), bf16)
    inv = jax.ShapeDtypeStruct((HF // Q, Q, Q), bf16)
    vmem = pl.BlockSpec(memory_space=pltpu.VMEM)
    return pl.pallas_call(
        kernel,
        name=name,
        out_shape=(part, part, inv, inv) + extra_out,
        in_specs=[pl.BlockSpec(memory_space=pltpu.SMEM) if a.dtype == jnp.int32 else vmem for a in args],
        out_specs=(vmem,) * (4 + len(extra_out)),
        scratch_shapes=[
            pltpu.VMEM((HF, width), bf16),
            pltpu.VMEM((HF, width), bf16),
            pltpu.VMEM((width, width), f32),
            pltpu.VMEM((B, 2 * B), f32),
            pltpu.VMEM((2, B, B), f32),
        ],
        compiler_params=pltpu.CompilerParams(vmem_limit_bytes=58 * MB),
        cost_estimate=pl.CostEstimate(flops=25_000_000_000, transcendentals=0, bytes_accessed=8 * MB),
    )(*args)


def chol_head(at, pieces):
    nxt = jax.ShapeDtypeStruct((HF, HF), f32)
    return chol_call(chol_head_kernel, "chol_head", PB, (nxt,), [at, *pieces])


def chol_tail(nxt):
    return chol_call(chol_tail_kernel, "chol_tail", HF, (), [nxt])


def finish_kernel(at_ref, w0, w1, w2, w3, pan, trail,
                  lh1, ll1, ih1, il1, lh2, ll2, ih2, il2,
                  fac_out, out_out,
                  a_ref, p_ref, t_ref, lh, ll, ih, il, xh, xl, wh, wl,
                  fac_ref, out_ref, sem, pan_sem, trail_sem, out_sem):
    row = at_ref[0]
    col = at_ref[1]
    copy = pltpu.make_async_copy
    lo, hi = pl.ds(0, HF), pl.ds(HF, HF)
    factors = [
        copy(ih1, ih.at[pl.ds(0, 2)], sem.at[0]), copy(il1, il.at[pl.ds(0, 2)], sem.at[1]),
        copy(lh1, lh.at[:, lo], sem.at[2]), copy(ll1, ll.at[:, lo], sem.at[3]),
        copy(ih2, ih.at[pl.ds(2, 2)], sem.at[4]), copy(il2, il.at[pl.ds(2, 2)], sem.at[5]),
        copy(lh2, lh.at[hi, hi], sem.at[6]), copy(ll2, ll.at[hi, hi], sem.at[7]),
    ]
    window = []
    for k in range(8):
        here = pl.ds(pl.multiple_of(jnp.bitwise_xor(row, k) * B, B), B)
        window.append(copy((w0, w1, w2, w3)[k // 2].at[k % 2], a_ref.at[here], sem.at[8 + k]))
    def panel_copy(n):
        return copy(pan.at[:, pl.ds(n * 512, 512)], p_ref.at[n], pan_sem.at[n])

    def trail_copy(n):
        return copy(trail.at[pl.ds(n * 512, 512)], t_ref.at[n], trail_sem.at[n])

    def fac_copy(n):
        return copy(fac_ref.at[n], fac_out.at[:, pl.ds(n * 512, 512)], out_sem.at[n])

    def out_copy(n):
        return copy(out_ref.at[n], out_out.at[pl.ds(n * 512, 512)], out_sem.at[3 + n])

    for d in factors[:2] + window + factors[2:]:
        d.start()
    panel_copy(0).start()
    for n in range(3):
        if n:
            panel_copy(n).start()
        trail_copy(n).start()

    def solve(src, yh, yl, needs=((),) * 4):
        for k in range(PB // Q):
            for d in needs[k]:
                d.wait()
            here = slice(k * Q, (k + 1) * Q)
            v = src[here, :]
            if k:
                v = v - dot3((lh[here, :k * Q], ll[here, :k * Q]), (yh[:k * Q, :], yl[:k * Q, :]))
            yh[here, :], yl[here, :] = split(dot3((ih[k], il[k]), split(v)))

    solve(a_ref, wh, wl, (factors[:2] + window, factors[2:4], factors[4:6], factors[6:]))
    mine = pl.ds(pl.multiple_of(col * PC, PC), PC)

    def block(n, _):
        panel_copy(n).wait()
        own = jnp.logical_and(row == 0, n < 2)

        @pl.when(own)
        def _():
            here = pl.ds(pl.multiple_of(n * 512, 512), 512)
            xh[...] = lh[here, :].T
            xl[...] = ll[here, :].T

        @pl.when(jnp.logical_and(row == 0, n == 0))
        def _():
            xh[HF:, :] = jnp.zeros((HF, 512), bf16)
            xl[HF:, :] = jnp.zeros((HF, 512), bf16)

        @pl.when(jnp.logical_not(own))
        def _():
            solve(p_ref.at[n], xh, xl)

        fac_ref[n] = xh[mine, :].astype(f32) + xl[mine, :].astype(f32)
        fac_copy(n).start()
        prod = dot3((xh[...], xl[...]), (wh[...], wl[...]), LHS_T)
        trail_copy(n).wait()
        out_ref[n] = t_ref[n] - prod
        out_copy(n).start()
        return 0

    lax.fori_loop(0, 3, block, 0)
    for n in range(3):
        fac_copy(n).wait()
        out_copy(n).wait()


def finish(at, window, panel, trail, head, tail):
    hbm = pl.BlockSpec(memory_space=pl.ANY)
    dma = pltpu.SemaphoreType.DMA
    vm = pltpu.VMEM
    return pl.pallas_call(
        finish_kernel,
        name="finish",
        out_shape=(jax.ShapeDtypeStruct((PC, FR), f32), jax.ShapeDtypeStruct((FR, TC), f32)),
        in_specs=[pl.BlockSpec(memory_space=pltpu.SMEM)] + [hbm] * 14,
        out_specs=(hbm, hbm),
        scratch_shapes=[
            vm((PB, TC), f32), vm((3, PB, 512), f32), vm((3, 512, TC), f32),
            vm((PB, PB), bf16), vm((PB, PB), bf16),
            vm((PB // Q, Q, Q), bf16), vm((PB // Q, Q, Q), bf16),
            vm((PB, 512), bf16), vm((PB, 512), bf16), vm((PB, TC), bf16), vm((PB, TC), bf16),
            vm((3, PC, 512), f32), vm((3, 512, TC), f32),
            dma((16,)), dma((3,)), dma((3,)), dma((6,)),
        ],
        compiler_params=pltpu.CompilerParams(vmem_limit_bytes=58 * MB),
        cost_estimate=pl.CostEstimate(flops=15_000_000_000, transcendentals=0, bytes_accessed=25 * MB),
    )(at, *window, panel, trail, *head, *tail)


def flip(x, axis, bit, size):
    return lax.ppermute(x, axis, [(i, i ^ bit) for i in range(size)])


def window_pairs(step):
    pairs = []
    for c in range(16):
        for parity in range(2):
            if ((c + 2) % 3 + parity) % 3 == step:
                for r in range(8):
                    pairs.append((((c + 2) // 3) * 16 + 2 * r + parity, r * 16 + c))
    return pairs


def on_device(front_panel, front_trail, child_panel, child_trail, child_map, child_count):
    row = lax.axis_index("row")
    col = lax.axis_index("col")
    at = jnp.stack([row, col]).astype(jnp.int32)

    count = child_count.T
    own, send, crit = panel_parts(
        at, count, child_map, front_panel.T, child_panel.transpose(0, 2, 1)
    )
    there = lax.ppermute(crit, "row", [(0, 4), (4, 0)])
    there, send = lax.optimization_barrier((there, send))
    got = flip(send, "row", 4, 8)
    diag = crit + there
    lo, hi = diag[:, :512], diag[:, 512:]
    half = jnp.where(row % 4 == 0, lo, 0.0)
    for k, part in ((1, hi), (2, lo), (3, hi)):
        half = half + lax.ppermute(part, "row", [(0, k), (4, 4 + k)])
    x4 = jnp.stack([half] + [flip(half, "col", b, 16) for b in (1, 2, 3)])
    x4, got, count, child_a = lax.optimization_barrier((x4, got, count, child_trail[1, :EA]))
    child_a = flip(child_a, "row", 4, 8)
    mine = [x4] + [flip(x4, "col", b, 16) for b in (4, 8, 12)]
    panel_t = own + got[:PC]
    odd = jnp.bitwise_and(col, 1)
    panes = [panel_t[:, 512 * w:512 * (w + 1)] for w in range(3)]
    picks = [jnp.where(odd == 0, panes[k], panes[(k + 2) % 3]) for k in range(3)]
    trail = trail_own(count, child_map, front_trail, child_trail)
    *mine, panel_t, trail, child_a, child_b, p0, p1, p2 = lax.optimization_barrier(
        (*mine, panel_t, trail, child_a, child_trail[1, EA:], *picks)
    )
    panel_full = lax.all_gather(panel_t, "col", axis=0, tiled=True)
    other = [flip(piece, "row", 1, 8) for piece in mine]
    steps = [lax.ppermute(p, ("row", "col"), window_pairs(k)) for k, p in enumerate((p0, p1, p2))]
    child_b = flip(child_b, "row", 4, 8)

    *head, nxt = chol_head(at, mine + other)
    *steps, nxt, child_b = lax.optimization_barrier((*steps, nxt, child_b))
    at_w = (col + 2) % 3
    first = jnp.where(at_w == 0, steps[0], jnp.where(at_w == 1, steps[1], steps[2]))
    second = jnp.where(at_w == 0, steps[1], jnp.where(at_w == 1, steps[2], steps[0]))
    win = jnp.concatenate([first, second], axis=0)
    pair = jnp.stack([win, flip(win, "row", 1, 8)])
    window = [pair] + [flip(pair, "row", b, 8) for b in (2, 4, 6)]
    tail = chol_tail(nxt)

    trail = trail_got(got, trail, child_a, child_b)
    factor_t, schur = finish(at, window, panel_full, trail, head, tail)
    return factor_t.T, schur


def solution(mesh):
    in_specs = (
        P("row", "col"),
        P("row", "col"),
        P(None, "row", "col"),
        P(None, "row", "col"),
        P(None, "row"),
        P(None, "row"),
    )
    out_specs = (P("row", "col"), P("row", "col"))
    return jax.shard_map(
        on_device, mesh=mesh, in_specs=in_specs, out_specs=out_specs, check_vma=False
    )
```
